128 devices in a mesh: bx: 16 (over x, y), by: 8 (over z, core).
Axes of the slice: x: 4, y: 4, z: 4, core: 2. Of those that a mesh axis runs over, the one named last changes fastest.
Arguments:
- tendency: bfloat16 [1536, 40, 64, 128], P(('bx', 'by')), may hold values from -6 to 6
- thickness: float32 [40], replicated, may hold values from 0.04 to 0.25
- depth: float32 [2048, 8192], P('by', 'bx'), may hold values from 0.25 to 1
- block_owner: int32 [1536], replicated, may hold values from 0 to 2047, as said below
- block_mask: int32 [32, 64], P('by', 'bx'), may hold values from 0 to 1, as said below
- ocean_counts: int32 [32, 64], P('by', 'bx'), may hold values from 0 to 8192, as said below
Outputs:
- heights: float32 [1536, 64, 128], P(('bx', 'by'))
The draws below stay inside these ranges and needn't reach their ends.
Inputs may be any that keep to these rules, and one draw needn't show every extreme that they name: `block_owner`: distinct grid blocks. Device t (index over bx+by with bx slowest; index i along bx, j along by) owns the region of block rows j * 4 to j * 4 + 3 and block columns i * 4 to i * 4 + 3; its slots t * 12 to t * 12 + 11 name blocks of its own region except 1 to 2 of its last 2 slots, which name blocks of the region of device (t + k) modulo 128 for one k of 1 to 2. Some device has 2 such slots with k = 2. `block_mask`: 1 exactly on the blocks that block_owner names. `ocean_counts`: 0 on land blocks; on ocean blocks from 2048 to 8192, and every region has a block with 8192.
All inputs are finite; a program needn't handle non-finite values.
Results may differ from the reference program's by a relative error of at most 0.0003.
Values sent between devices are 32-bit elements; how exact they have to be, the bound alone decides.
No kernel may reach another device: no remote copies, remote signals or barrier semaphores. Data moves between devices by JAX's collectives and lax.ppermute only.
A program may use at most 64 MiB of HBM per device.

```python
import math
import jax
import jax.numpy as jnp
from jax import lax

BLOCK_ROWS = 64
BLOCK_COLUMNS = 128
TBY = 4
TBX = 4
CB = 12
MOVE = 2
REACH = 2
LAYER_COUNT = 40
ITERS = 10
NDEV = 128
SLOT_COUNT = 1536
NBY = 32
NBX = 64
NY = 2048
NX = 8192


def layout(key):
    region = TBY * TBX
    cells = BLOCK_ROWS * BLOCK_COLUMNS
    rows_axis = NBY // TBY
    inflow = jax.random.randint(jax.random.fold_in(key, 11), (NDEV,), 1, MOVE + 1).astype(jnp.int32).at[0].set(MOVE)
    offsets = jax.random.randint(jax.random.fold_in(key, 12), (NDEV,), 1, REACH + 1).astype(jnp.int32).at[0].set(REACH)
    devices = jnp.arange(NDEV, dtype=jnp.int32)
    target = (devices + offsets) % NDEV
    staying = CB - inflow
    arriving = jax.ops.segment_sum(inflow, target, num_segments=NDEV)
    capacity = staying + arriving
    same_target = (target[:, None] == target[None, :]) & (devices[None, :] < devices[:, None])
    before = jnp.sum(jnp.where(same_target, inflow[None, :], 0), axis=1)
    first_rank = staying[target] + before
    scores = jax.random.randint(jax.random.fold_in(key, 13), (NDEV, region), 0, 1 << 20).astype(jnp.int32) * region + jnp.arange(region, dtype=jnp.int32)[None, :]
    ordering = jnp.argsort(scores, axis=1).astype(jnp.int32)
    ranking = jnp.argsort(ordering, axis=1).astype(jnp.int32)
    slot_index = jnp.arange(CB, dtype=jnp.int32)[None, :]
    moved = slot_index >= staying[:, None]
    holder_region = jnp.where(moved, target[:, None], devices[:, None])
    holder_rank = jnp.where(moved, first_rank[:, None] + slot_index - staying[:, None], slot_index)
    local_block = ordering[holder_region, holder_rank]
    grid_row = holder_region % rows_axis * TBY + local_block // TBX
    grid_col = holder_region // rows_axis * TBX + local_block % TBX
    owners = (grid_row * NBX + grid_col).reshape(-1).astype(jnp.int32)
    wet_blocks = (ranking < capacity[:, None]).astype(jnp.int32)
    fullness = jax.random.randint(jax.random.fold_in(key, 14), (NDEV, region), cells // 4, cells + 1).astype(jnp.int32)
    fullness = jnp.where(ranking == 0, cells, fullness) * wet_blocks
    return (owners, wet_blocks, fullness)


def territory_grid(values):
    rows_axis = NBY // TBY
    cols_axis = NBX // TBX
    return values.reshape(cols_axis, rows_axis, TBY, TBX).transpose(1, 2, 0, 3).reshape(NBY, NBX)


def draw_block_owner(key, part):
    owners, wet_blocks, fullness = layout(key)
    return owners


def draw_block_mask(key, part):
    owners, wet_blocks, fullness = layout(key)
    return territory_grid(wet_blocks).astype(jnp.int32)


def draw_ocean_counts(key, part):
    owners, wet_blocks, fullness = layout(key)
    return territory_grid(fullness).astype(jnp.int32)


def draw_tendency(key, part):
    array_extent = (SLOT_COUNT, LAYER_COUNT, BLOCK_ROWS, BLOCK_COLUMNS)
    values = jax.random.normal(key, array_extent, jnp.float32)
    return jnp.clip(values, -6.0, 6.0).astype(jnp.bfloat16)


def levels(own_key, shape, pieces, least, top_value):
    factor_of = 1.0
    for dim, parts in pieces:
        draws = jax.random.uniform(jax.random.fold_in(jax.random.fold_in(own_key, 6), dim), (parts,), jnp.float32, least / len(pieces), top_value / len(pieces))
        factor_of = factor_of * jnp.repeat(jnp.exp(draws), shape[dim] // parts).reshape((-1,) + (1,) * (len(shape) - 1 - dim))
    return factor_of


def setup_inputs(seed: int = 0) -> dict:
    key_of = jax.random.split(jax.random.key(seed), 7)
    return {
        "tendency": draw_tendency(jax.random.fold_in(key_of[6], 71), 0),
        "thickness": jnp.clip(jnp.exp(jax.random.uniform(key_of[1], (LAYER_COUNT,), jnp.float32, math.log(0.04), math.log(0.25))), 0.04, 0.25),
        "depth": jnp.clip(jnp.exp(math.log(1.0) - 1.3862944 * jax.random.uniform(key_of[2], (NY, NX), jnp.float32) ** levels(key_of[2], (NY, NX), ((0, 8), (1, 16)), -0.2, 0.2)), 0.25, 1.0),
        "block_owner": draw_block_owner(jax.random.fold_in(key_of[6], 71), 0),
        "block_mask": draw_block_mask(jax.random.fold_in(key_of[6], 71), 0),
        "ocean_counts": draw_ocean_counts(jax.random.fold_in(key_of[6], 71), 0),
    }


surface_term = 0.1
lower_bound = 0.05
upper_bound = 2.0


def chebyshev_plan():
    centre_value = (upper_bound + lower_bound) / 2.0
    half_width = (upper_bound - lower_bound) / 2.0
    ratio_value = centre_value / half_width
    weight = 1.0 / ratio_value
    scales = []
    for sweep in range(ITERS):
        renewed = 1.0 / (2.0 * ratio_value - weight)
        scales.append((renewed * weight, 2.0 * renewed / half_width))
        weight = renewed
    return 1.0 / centre_value, scales


def corners(padded):
    return jnp.minimum(jnp.minimum(padded[:-1, :-1], padded[:-1, 1:]), jnp.minimum(padded[1:, :-1], padded[1:, 1:]))


def beside_all(values):
    return values[:-1, :-1] + values[:-1, 1:] + values[1:, :-1] + values[1:, 1:]


def operate(padded, corner_depth):
    corner_mean = 0.25 * beside_all(padded)
    centre = padded[1:-1, 1:-1]
    return surface_term * centre + beside_all(corner_depth) * centre - beside_all(corner_depth * corner_mean)


def pad_grid(field_values):
    wrapped = jnp.concatenate([field_values[:, -1:], field_values, field_values[:, :1]], axis=1)
    return jnp.pad(wrapped, ((1, 1), (0, 0)))


def to_grid(blocks):
    return blocks.reshape(NBY, NBX, BLOCK_ROWS, BLOCK_COLUMNS).transpose(0, 2, 1, 3).reshape(NY, NX)


def to_blocks(field_values):
    return field_values.reshape(NBY, BLOCK_ROWS, NBX, BLOCK_COLUMNS).transpose(0, 2, 1, 3).reshape(NBY * NBX, BLOCK_ROWS, BLOCK_COLUMNS)


def reference(tendency, thickness, depth, block_owner, block_mask, ocean_counts):
    def column(column_slab):
        return jnp.sum(column_slab.astype(jnp.float32) * thickness[:, None, None], axis=0)

    forcing = lax.map(column, tendency)
    placed = jnp.zeros((NBY * NBX, BLOCK_ROWS, BLOCK_COLUMNS), jnp.float32).at[block_owner].set(forcing)
    forcing_grid = to_grid(placed)
    position = jnp.arange(BLOCK_ROWS, dtype=jnp.int32)[:, None] * BLOCK_COLUMNS + jnp.arange(BLOCK_COLUMNS, dtype=jnp.int32)[None, :]
    wetness = (position[None, None] < ocean_counts[:, :, None, None]) & (block_mask[:, :, None, None] == 1)
    oceanic = to_grid(wetness.astype(jnp.float32))
    masked_depth = depth * oceanic
    source = forcing_grid * oceanic
    corner_depth = corners(pad_grid(masked_depth))
    inverse = 1.0 / (surface_term + 0.75 * beside_all(corner_depth))
    opening, scales = chebyshev_plan()
    solution = jnp.zeros_like(source)
    residual = source
    direction = opening * (inverse * residual)
    for sweep in range(ITERS):
        carry_scale, forward_scale = scales[sweep]
        applied = operate(pad_grid(direction), corner_depth)
        solution = solution + direction
        residual = residual - applied
        if sweep + 1 < ITERS:
            direction = carry_scale * direction + forward_scale * (inverse * residual)
    return to_blocks(solution)[block_owner]
```

```python
import functools

import jax
import jax.numpy as jnp
from jax import lax
from jax.experimental import pallas as pl
from jax.experimental.pallas import tpu as pltpu
from jax.sharding import PartitionSpec as P

MOVE = 2
ITERS = 10
ROWS, LANES = 64, 128
SLOTS = 12
KEPT = SLOTS - MOVE
LEVELS = 40
REGION = 4
OWN_ROWS = REGION * ROWS
CHUNK = 35
EXT_ROWS = 8 * CHUNK
FOLD = 72
PACK_ROWS = 4 * FOLD
COLS = REGION + 1

surface_term = 0.1
lower_bound = 0.05
upper_bound = 2.0

VMEM = pltpu.MemorySpace.VMEM
SMEM = pltpu.MemorySpace.SMEM


def chebyshev_plan():
    centre_value = (upper_bound + lower_bound) / 2.0
    half_width = (upper_bound - lower_bound) / 2.0
    ratio_value = centre_value / half_width
    weight = 1.0 / ratio_value
    scales = []
    for sweep in range(ITERS):
        renewed = 1.0 / (2.0 * ratio_value - weight)
        scales.append((renewed * weight, 2.0 * renewed / half_width))
        weight = renewed
    return (1.0 / centre_value, scales)


def place(block):
    row, col = block // 64, block % 64
    return (col // REGION) * 8 + row // REGION, row % REGION, col % REGION


def rolled(value, steps, axis):
    return pltpu.roll(value, steps % value.shape[axis], axis)


def column_sum(tend_ref, thick_ref):
    out = []
    for tile in range(ROWS // 16):
        total = jnp.zeros((16, LANES), jnp.float32)
        for level in range(LEVELS):
            part = tend_ref[0, level, tile * 16 : tile * 16 + 16, :].astype(jnp.float32)
            total = total + part * thick_ref[level]
        out.append(total)
    return out


def moved_kernel(thick_ref, tend_ref, moved_ref, bottom_ref):
    tiles = column_sum(tend_ref, thick_ref)
    for tile, value in enumerate(tiles):
        moved_ref[0, tile * 16 : tile * 16 + 16, :] = value
    bottom_ref[0] = tiles[-1]


def wetness(rows, first_row, count, mask):
    position = (lax.broadcasted_iota(jnp.int32, (rows, LANES), 0) + first_row) * LANES + (
        lax.broadcasted_iota(jnp.int32, (rows, LANES), 1)
    )
    return (position < count) & (mask == 1)


def kept_kernel(
    thick_ref, owner_ref, count_ref, mask_ref, tend_ref, moved_ref, head_ref, tail_ref,
    kept_ref, up_ref, down_ref,
):
    step = pl.program_id(0)
    myself = lax.axis_index("bx") * 8 + lax.axis_index("by")

    def edges(slot, top, bottom):
        region, row, col = place(owner_ref[myself * SLOTS + slot])
        lanes = pl.ds(pl.multiple_of(col * LANES, LANES), LANES)

        @pl.when((region == myself) & (row == 0))
        def _():
            up_ref[16:32, lanes] = top

        @pl.when((region == myself) & (row == REGION - 1))
        def _():
            down_ref[16:32, lanes] = bottom

    @pl.when(step == 0)
    def _():
        up_ref[16:32, :] = jnp.zeros((16, REGION * LANES), jnp.float32)
        down_ref[16:32, :] = jnp.zeros((16, REGION * LANES), jnp.float32)
        for col in range(REGION):
            lanes = slice(col * LANES, (col + 1) * LANES)
            wet = wetness(16, 0, count_ref[0, col], mask_ref[0, col])
            up_ref[0:16, lanes] = jnp.where(wet, head_ref[:, lanes], 0.0)
            wet = wetness(16, ROWS - 16, count_ref[REGION - 1, col], mask_ref[REGION - 1, col])
            down_ref[0:16, lanes] = jnp.where(wet, tail_ref[:, lanes], 0.0)
        for extra in range(MOVE):
            edges(KEPT + extra, moved_ref[extra, 0:16, :], moved_ref[extra, 48:64, :])

    tiles = column_sum(tend_ref, thick_ref)
    for tile, value in enumerate(tiles):
        kept_ref[0, tile * 16 : tile * 16 + 16, :] = value
    edges(step, tiles[0], tiles[-1])


def gather_kernel(
    owner_ref, count_ref, mask_ref, depth_ref, kept_ref, moved_ref, one_ref, two_ref, three_ref,
    north_ref, south_ref,
    source_ref, masked_ref, left_ref, right_ref,
):
    row_index = lax.axis_index("by")
    myself = lax.axis_index("bx") * 8 + row_index
    end = OWN_ROWS + 8
    lane = lax.broadcasted_iota(jnp.int32, (8, LANES), 1)
    upper = lax.broadcasted_iota(jnp.int32, (8, LANES), 0) < 4

    not_south = row_index == 7
    not_north = row_index == 0
    for col in range(REGION):
        lanes = slice(col * LANES, (col + 1) * LANES)
        for row in range(REGION):
            rows = slice(row * ROWS, (row + 1) * ROWS)
            wet = wetness(ROWS, 0, count_ref[row, col], mask_ref[row, col])
            masked_ref[col, rows, :] = jnp.where(wet, depth_ref[rows, lanes], 0.0)
        south = [jnp.where(not_south, 0.0, south_ref[8 * i : 8 * i + 8, lanes]) for i in range(2)]
        north = [jnp.where(not_north, 0.0, north_ref[8 * i : 8 * i + 8, lanes]) for i in range(2)]
        masked_ref[col, OWN_ROWS:end, :] = south[0]
        masked_ref[col, end : end + 8, :] = jnp.where(upper, south[1], north[0])
        masked_ref[col, end + 8 : end + 16, :] = north[1]
        masked_ref[col, EXT_ROWS:PACK_ROWS, :] = jnp.zeros((8, LANES), jnp.float32)
        source_ref[col, 0:OWN_ROWS, :] = jnp.zeros((OWN_ROWS, LANES), jnp.float32)
        source_ref[col, OWN_ROWS:end, :] = south_ref[16:24, lanes]
        source_ref[col, end : end + 8, :] = jnp.where(
            upper, south_ref[24:32, lanes], north_ref[16:24, lanes]
        )
        source_ref[col, end + 8 : end + 16, :] = north_ref[24:32, lanes]
        source_ref[col, EXT_ROWS:PACK_ROWS, :] = jnp.zeros((8, LANES), jnp.float32)

    def spread(sender, slot, block, bottom, inside=True, above=True, below=True):
        region, row, col = place(owner_ref[sender * SLOTS + slot])
        if inside:

            @pl.when(region == myself)
            def _():
                first = pl.multiple_of(row * ROWS, ROWS)
                source_ref[col, pl.ds(first, ROWS), :] = block[...]

        if below:

            @pl.when((region == myself + 1) & (row == 0))
            def _():
                source_ref[col, OWN_ROWS:end, :] = block[0:8, :]
                mixed = source_ref[col, end : end + 8, :]
                source_ref[col, end : end + 8, :] = jnp.where(upper, block[8:16, :], mixed)

        if above:

            @pl.when((region == myself - 1) & (row == REGION - 1))
            def _():
                mixed = source_ref[col, end : end + 8, :]
                source_ref[col, end : end + 8, :] = jnp.where(upper, mixed, bottom[0:8, :])
                source_ref[col, end + 8 : end + 16, :] = bottom[8:16, :]

    for slot in range(KEPT):
        spread(myself, slot, kept_ref.at[slot], None, above=False, below=False)
    for extra in range(MOVE):
        slot = KEPT + extra
        block = moved_ref.at[extra]
        spread(myself, slot, block, None, above=False)
        block = one_ref.at[extra]
        spread((myself + 127) % 128, slot, block, None, above=False)
        block = two_ref.at[extra]
        spread((myself + 126) % 128, slot, block, block.at[48:64, :], below=False)
        spread((myself + 125) % 128, slot, None, three_ref.at[extra], inside=False, below=False)

    for col in range(REGION):
        for row in range(PACK_ROWS // 8):
            rows = slice(row * 8, row * 8 + 8)
            value = source_ref[col, rows, :]
            source_ref[col, rows, :] = jnp.where(masked_ref[col, rows, :] > 0.0, value, 0.0)

    for row in range(FOLD // 8):
        left = jnp.zeros((8, LANES), jnp.float32)
        right = jnp.zeros((8, LANES), jnp.float32)
        for group in range(4):
            rows = slice(group * FOLD + row * 8, group * FOLD + row * 8 + 8)
            for field, ref in enumerate((masked_ref, source_ref)):
                to = 32 * group + 16 * field
                here = (lane >= to) & (lane < to + 16)
                left = jnp.where(here, rolled(ref[0, rows, :], to, 1), left)
                right = jnp.where(here, rolled(ref[REGION - 1, rows, :], to + 16, 1), right)
        left_ref[row * 8 : row * 8 + 8, :] = left
        right_ref[row * 8 : row * 8 + 8, :] = right


def solve_kernel(
    owner_ref, source_ref, masked_ref, west_ref, east_ref,
    out_ref, one_ref, two_ref,
    side, direction, residual, total, corner, inverse, diagonal, standard,
):
    myself = lax.axis_index("bx") * 8 + lax.axis_index("by")
    lane = lax.broadcasted_iota(jnp.int32, (8, LANES), 1)
    first_lane, last_lane = lane == 0, lane == LANES - 1
    opening, scales = chebyshev_plan()

    for group in range(4):
        for row in range(FOLD // 8):
            rows = slice(row * 8, row * 8 + 8)
            west, east = west_ref[rows, :], east_ref[rows, :]
            for field in range(2):
                start = 32 * group + 16 * field
                value = jnp.where(lane < 16, rolled(east, -start, 1), 0.0)
                value = jnp.where(lane >= 112, rolled(west, 112 - start, 1), value)
                first = group * FOLD + row * 8
                side[field, first : first + 8, :] = value

    def strided(ref, field, k):
        rows = pl.ds(k, 8, stride=CHUNK)
        return [ref[col, rows, :] for col in range(REGION)] + [side[field, rows, :]]

    def from_west(row):
        turned = [rolled(value, 1, 1) for value in row]
        return [jnp.where(first_lane, turned[c - 1], turned[c]) for c in range(COLS)]

    def from_east(row):
        turned = [rolled(value, -1, 1) for value in row]
        return [jnp.where(last_lane, turned[(c + 1) % COLS], turned[c]) for c in range(COLS)]

    def join(f, *rows):
        return [f(*values) for values in zip(*rows)]

    def down(row):
        return [rolled(value, 1, 0) for value in row]

    def up(row):
        return [rolled(value, -1, 0) for value in row]

    def load(ref, k):
        return [ref[k, col] for col in range(COLS)]

    def store(ref, k, row):
        for col in range(COLS):
            ref[k, col] = row[col]

    def corner_depth(above, here):
        both = join(jnp.minimum, above, here)
        return join(jnp.minimum, both, from_west(both))

    def gathered(row):
        return join(jnp.add, row, from_east(row))

    here = strided(masked_ref, 1 - 1, 0)
    first_corner = corner_depth(down(strided(masked_ref, 0, CHUNK - 1)), here)
    below_last = up(first_corner)

    def prepare(k, carry):
        here, above_corner = carry
        following = strided(masked_ref, 0, jnp.minimum(k + 1, CHUNK - 1))
        under = corner_depth(here, following)
        last = k == CHUNK - 1
        under = join(lambda a, b: jnp.where(last, b, a), under, below_last)
        around = gathered(join(jnp.add, above_corner, under))
        source = strided(source_ref, 1, k)
        for col in range(COLS):
            inv = 1.0 / (surface_term + 0.75 * around[col])
            start = inv * source[col]
            inverse[k, col] = inv
            diagonal[k, col] = inv * (surface_term + around[col])
            corner[k, col] = 0.25 * above_corner[col]
            residual[k, col] = start
            direction[k, col] = opening * start
            total[k, col] = jnp.zeros((8, LANES), jnp.float32)
        return tuple(following), tuple(under)

    lax.fori_loop(0, CHUNK, prepare, (tuple(here), tuple(first_corner)))

    def flux(above, here, k):
        both = join(jnp.add, above, here)
        spread = join(jnp.add, both, from_west(both))
        return join(jnp.multiply, spread, load(corner, k))

    for sweep in range(ITERS - 1):
        carry_scale, forward_scale = scales[sweep]
        final = sweep == ITERS - 2
        first_row = load(direction, 0)
        first_flux = flux(down(load(direction, CHUNK - 1)), first_row, 0)
        below_last = up(first_flux)

        def advance(k, here, flux_above, following, flux_below):
            back = gathered(join(jnp.add, flux_above, flux_below))
            for col in range(COLS):
                rest = residual[k, col] - diagonal[k, col] * here[col] + inverse[k, col] * back[col]
                turned = carry_scale * here[col] + forward_scale * rest
                summed = total[k, col] + here[col]
                if final:
                    if col < REGION:
                        standard[col, pl.ds(k, 8, stride=CHUNK), :] = summed + turned
                else:
                    residual[k, col] = rest
                    direction[k, col] = turned
                    total[k, col] = summed

        def body(k, carry):
            here, flux_above = carry
            following = load(direction, k + 1)
            flux_below = flux(here, following, k + 1)
            advance(k, here, flux_above, following, flux_below)
            return tuple(following), tuple(flux_below)

        here, flux_above = lax.fori_loop(
            0, CHUNK - 1, body, (tuple(first_row), tuple(first_flux)), unroll=2
        )
        advance(CHUNK - 1, here, flux_above, None, below_last)

    def answer(sender, slot, ref, index):
        region, row, col = place(owner_ref[sender * SLOTS + slot])
        mine = region == myself
        first = pl.multiple_of(row * ROWS, ROWS)
        value = standard[col, pl.ds(first, ROWS), :]
        ref[index] = jnp.where(mine, value, 0.0)

    for extra in range(MOVE):
        answer((myself + 127) % 128, KEPT + extra, one_ref, extra)
        answer((myself + 126) % 128, KEPT + extra, two_ref, extra)
    for slot in range(SLOTS):
        answer(myself, slot, out_ref, slot)


def whole(space=VMEM):
    return pl.BlockSpec(memory_space=space)


def ring(value, steps):
    count = lax.axis_size("bx") * lax.axis_size("by")
    return lax.ppermute(value, ("bx", "by"), [(i, (i + steps) % count) for i in range(count)])


def along(value, axis, steps):
    count = lax.axis_size(axis)
    return lax.ppermute(value, axis, [(i, (i + steps) % count) for i in range(count)])


def on_device(tendency, thickness, depth, block_owner, block_mask, ocean_counts):
    f32 = jnp.float32

    def shape(*dims):
        return jax.ShapeDtypeStruct(dims, f32)

    moved, bottom = pl.pallas_call(
        moved_kernel,
        grid=(MOVE,),
        in_specs=[
            whole(SMEM),
            pl.BlockSpec((1, LEVELS, ROWS, LANES), lambda i: (KEPT + i, 0, 0, 0)),
        ],
        out_specs=[
            pl.BlockSpec((1, ROWS, LANES), lambda i: (i, 0, 0)),
            pl.BlockSpec((1, 16, LANES), lambda i: (i, 0, 0)),
        ],
        out_shape=[shape(MOVE, ROWS, LANES), shape(MOVE, 16, LANES)],
        name="moved_forcing",
    )(thickness, tendency)
    one, two, three = ring(moved, 1), ring(moved, 2), ring(bottom, 3)

    edge = pl.BlockSpec((16, REGION * LANES), lambda i: (0, 0))
    kept, upper, lower = pl.pallas_call(
        kept_kernel,
        grid=(KEPT,),
        in_specs=[
            whole(SMEM), whole(SMEM), whole(SMEM), whole(SMEM),
            pl.BlockSpec((1, LEVELS, ROWS, LANES), lambda i: (i, 0, 0, 0)),
            pl.BlockSpec((MOVE, ROWS, LANES), lambda i: (0, 0, 0)),
            edge,
            pl.BlockSpec((16, REGION * LANES), lambda i: (OWN_ROWS // 16 - 1, 0)),
        ],
        out_specs=[
            pl.BlockSpec((1, ROWS, LANES), lambda i: (i, 0, 0)),
            pl.BlockSpec((32, REGION * LANES), lambda i: (0, 0)),
            pl.BlockSpec((32, REGION * LANES), lambda i: (0, 0)),
        ],
        out_shape=[
            shape(KEPT, ROWS, LANES),
            shape(32, REGION * LANES),
            shape(32, REGION * LANES),
        ],
        name="kept_forcing",
    )(thickness, block_owner, ocean_counts, block_mask, tendency, moved, depth, depth)
    north = along(lower, "by", 1)
    south = along(upper, "by", -1)

    source, masked, left, right = pl.pallas_call(
        gather_kernel,
        in_specs=[whole(SMEM)] * 3 + [whole()] * 8,
        out_specs=[whole()] * 4,
        out_shape=[
            shape(REGION, PACK_ROWS, LANES),
            shape(REGION, PACK_ROWS, LANES),
            shape(FOLD, LANES),
            shape(FOLD, LANES),
        ],
        name="assemble",
    )(block_owner, ocean_counts, block_mask, depth, kept, moved, one, two, three, north, south)
    west = along(right, "bx", 1)
    east = along(left, "bx", -1)

    field = pltpu.VMEM((CHUNK, COLS, 8, LANES), f32)
    heights, first, second = pl.pallas_call(
        solve_kernel,
        in_specs=[whole(SMEM)] + [whole()] * 4,
        out_specs=[whole()] * 3,
        out_shape=[shape(SLOTS, ROWS, LANES), shape(MOVE, ROWS, LANES), shape(MOVE, ROWS, LANES)],
        scratch_shapes=[pltpu.VMEM((2, PACK_ROWS, LANES), f32)]
        + [field] * 6
        + [pltpu.VMEM((REGION, EXT_ROWS, LANES), f32)],
        compiler_params=pltpu.CompilerParams(vmem_limit_bytes=32 << 20),
        name="solve",
    )(block_owner, source, masked, west, east)
    back = ring(first, -1) + ring(second, -2)
    return heights.at[KEPT:].add(back)


def solution(mesh):
    placed = (
        P(("bx", "by"), None, None, None),
        P(),
        P("by", "bx"),
        P(),
        P("by", "bx"),
        P("by", "bx"),
    )
    return jax.shard_map(
        on_device,
        mesh=mesh,
        in_specs=placed,
        out_specs=P(("bx", "by"), None, None),
        check_vma=False,
    )
```

```python
import jax
import jax.numpy as jnp
from jax import lax
from jax.experimental import pallas as pl
from jax.experimental.pallas import tpu as pltpu
from jax.sharding import PartitionSpec as P

MOVE = 2
ITERS = 10
ROWS, LANES = 64, 128
SLOTS = 12
KEPT = SLOTS - MOVE
LEVELS = 40
REGION = 4
OWN_ROWS = REGION * ROWS
CHUNK = 35
EXT_ROWS = 8 * CHUNK
FOLD = 72
PACK_ROWS = 4 * FOLD
COLS = REGION + 1

surface_term = 0.1
lower_bound = 0.05
upper_bound = 2.0

VMEM = pltpu.MemorySpace.VMEM
SMEM = pltpu.MemorySpace.SMEM
HBM = pltpu.MemorySpace.HBM


def chebyshev_plan():
    centre_value = (upper_bound + lower_bound) / 2.0
    half_width = (upper_bound - lower_bound) / 2.0
    ratio_value = centre_value / half_width
    weight = 1.0 / ratio_value
    scales = []
    for sweep in range(ITERS):
        renewed = 1.0 / (2.0 * ratio_value - weight)
        scales.append((renewed * weight, 2.0 * renewed / half_width))
        weight = renewed
    return (1.0 / centre_value, scales)


def place(block):
    row, col = block // 64, block % 64
    return (col // REGION) * 8 + row // REGION, row % REGION, col % REGION


def rolled(value, steps, axis):
    return pltpu.roll(value, steps % value.shape[axis], axis)


def wetness(rows, count, mask):
    position = lax.broadcasted_iota(jnp.int32, (rows, LANES), 0) * LANES + (
        lax.broadcasted_iota(jnp.int32, (rows, LANES), 1)
    )
    return (position < count) & (mask == 1)


def forcing_kernel(
    thick_in, owner_in, count_in, mask_in, tend_ref, depth_ref,
    moved_ref, bottom_ref, up_ref, down_ref, source_ref, masked_ref,
    thick_ref, owner_ref, count_ref, mask_ref, levels, sea, table_sem, level_sem, sea_sem,
):
    myself = lax.axis_index("bx") * 8 + lax.axis_index("by")
    tables = []
    for index, (table_in, table_ref) in enumerate(
        ((count_in, count_ref), (mask_in, mask_ref), (thick_in, thick_ref), (owner_in, owner_ref))
    ):
        copy = pltpu.make_async_copy(table_in, table_ref, table_sem.at[index])
        copy.start()
        tables.append(copy)
    sea_copy = pltpu.make_async_copy(depth_ref, sea, sea_sem)
    sea_copy.start()
    copies = []
    for slot in range(SLOTS):
        copy = pltpu.make_async_copy(tend_ref.at[slot], levels.at[slot], level_sem.at[slot])
        copy.start()
        copies.append(copy)

    width = REGION * LANES
    up_ref[16:32, :] = jnp.zeros((16, width), jnp.float32)
    down_ref[16:32, :] = jnp.zeros((16, width), jnp.float32)
    source_ref[...] = jnp.zeros(source_ref.shape, jnp.float32)
    for copy in tables:
        copy.wait()
    sea_copy.wait()
    for col in range(REGION):
        lanes = slice(col * LANES, (col + 1) * LANES)
        for row in range(REGION):
            rows = slice(row * ROWS, (row + 1) * ROWS)
            wet = wetness(ROWS, count_ref[row, col], mask_ref[row, col])
            value = jnp.where(wet, sea[rows, lanes], 0.0)
            masked_ref[col, rows, :] = value
            if row == 0:
                up_ref[0:16, lanes] = value[0:16, :]
            if row == REGION - 1:
                down_ref[0:16, lanes] = value[48:64, :]
        masked_ref[col, OWN_ROWS:PACK_ROWS, :] = jnp.zeros((PACK_ROWS - OWN_ROWS, LANES), jnp.float32)

    for slot in range(SLOTS):
        copies[slot].wait()
        totals = [jnp.zeros((16, LANES), jnp.float32) for _ in range(ROWS // 16)]
        for level in range(LEVELS):
            weight = thick_ref[level]
            for tile in range(ROWS // 16):
                part = levels[slot, level, tile * 16 : tile * 16 + 16, :].astype(jnp.float32)
                totals[tile] = totals[tile] + part * weight
        if slot >= KEPT:
            for tile, value in enumerate(totals):
                moved_ref[slot - KEPT, tile * 16 : tile * 16 + 16, :] = value
            bottom_ref[slot - KEPT] = totals[-1]
        region, row, col = place(owner_ref[myself * SLOTS + slot])
        lanes = pl.ds(pl.multiple_of(col * LANES, LANES), LANES)

        @pl.when(region == myself)
        def _():
            for tile, value in enumerate(totals):
                first = pl.multiple_of(row * ROWS + tile * 16, 16)
                source_ref[col, pl.ds(first, 16), :] = value

        @pl.when((region == myself) & (row == 0))
        def _():
            up_ref[16:32, lanes] = totals[0]

        @pl.when((region == myself) & (row == REGION - 1))
        def _():
            down_ref[16:32, lanes] = totals[-1]


def gather_kernel(
    owner_ref, source_in, masked_in, moved_ref, one_ref, two_ref, three_ref, north_ref, south_ref,
    source_ref, masked_ref, left_ref, right_ref,
):
    del source_in, masked_in
    row_index = lax.axis_index("by")
    myself = lax.axis_index("bx") * 8 + row_index
    end = OWN_ROWS + 8
    lane = lax.broadcasted_iota(jnp.int32, (8, LANES), 1)
    upper = lax.broadcasted_iota(jnp.int32, (8, LANES), 0) < 4

    not_south = row_index == 7
    not_north = row_index == 0
    for col in range(REGION):
        lanes = slice(col * LANES, (col + 1) * LANES)
        south = [jnp.where(not_south, 0.0, south_ref[8 * i : 8 * i + 8, lanes]) for i in range(2)]
        north = [jnp.where(not_north, 0.0, north_ref[8 * i : 8 * i + 8, lanes]) for i in range(2)]
        masked_ref[col, OWN_ROWS:end, :] = south[0]
        masked_ref[col, end : end + 8, :] = jnp.where(upper, south[1], north[0])
        masked_ref[col, end + 8 : end + 16, :] = north[1]
        source_ref[col, OWN_ROWS:end, :] = south_ref[16:24, lanes]
        source_ref[col, end : end + 8, :] = jnp.where(
            upper, south_ref[24:32, lanes], north_ref[16:24, lanes]
        )
        source_ref[col, end + 8 : end + 16, :] = north_ref[24:32, lanes]

    def spread(sender, slot, block, bottom, inside=True, above=True, below=True):
        region, row, col = place(owner_ref[sender * SLOTS + slot])
        if inside:

            @pl.when(region == myself)
            def _():
                first = pl.multiple_of(row * ROWS, ROWS)
                source_ref[col, pl.ds(first, ROWS), :] = block[...]

        if below:

            @pl.when((region == myself + 1) & (row == 0))
            def _():
                source_ref[col, OWN_ROWS:end, :] = block[0:8, :]
                mixed = source_ref[col, end : end + 8, :]
                source_ref[col, end : end + 8, :] = jnp.where(upper, block[8:16, :], mixed)

        if above:

            @pl.when((region == myself - 1) & (row == REGION - 1))
            def _():
                mixed = source_ref[col, end : end + 8, :]
                source_ref[col, end : end + 8, :] = jnp.where(upper, mixed, bottom[0:8, :])
                source_ref[col, end + 8 : end + 16, :] = bottom[8:16, :]

    for extra in range(MOVE):
        slot = KEPT + extra
        block = moved_ref.at[extra]
        spread(myself, slot, block, None, inside=False, above=False)
        block = one_ref.at[extra]
        spread((myself + 127) % 128, slot, block, None, above=False)
        block = two_ref.at[extra]
        spread((myself + 126) % 128, slot, block, block.at[48:64, :], below=False)
        spread((myself + 125) % 128, slot, None, three_ref.at[extra], inside=False, below=False)

    for row in range(FOLD // 8):
        left = jnp.zeros((8, LANES), jnp.float32)
        right = jnp.zeros((8, LANES), jnp.float32)
        for group in range(4):
            rows = slice(group * FOLD + row * 8, group * FOLD + row * 8 + 8)
            for field, ref in enumerate((masked_ref, source_ref)):
                to = 32 * group + 16 * field
                here = (lane >= to) & (lane < to + 16)
                left = jnp.where(here, rolled(ref[0, rows, :], to, 1), left)
                right = jnp.where(here, rolled(ref[REGION - 1, rows, :], to + 16, 1), right)
        left_ref[row * 8 : row * 8 + 8, :] = left
        right_ref[row * 8 : row * 8 + 8, :] = right


def solve_kernel(
    owner_ref, scale_ref, source_ref, masked_ref, west_ref, east_ref,
    standard, one_ref, two_ref,
    side, direction, residual, total, corner, inverse, diagonal, flow,
):
    myself = lax.axis_index("bx") * 8 + lax.axis_index("by")
    lane = lax.broadcasted_iota(jnp.int32, (8, LANES), 1)
    first_lane, last_lane = lane == 0, lane == LANES - 1
    opening, _ = chebyshev_plan()

    for group in range(4):
        for row in range(FOLD // 8):
            rows = slice(row * 8, row * 8 + 8)
            west, east = west_ref[rows, :], east_ref[rows, :]
            for field in range(2):
                start = 32 * group + 16 * field
                value = jnp.where(lane < 16, rolled(east, -start, 1), 0.0)
                value = jnp.where(lane >= 112, rolled(west, 112 - start, 1), value)
                first = group * FOLD + row * 8
                side[field, first : first + 8, :] = value

    def strided(ref, field, k):
        rows = pl.ds(k, 8, stride=CHUNK)
        return [ref[col, rows, :] for col in range(REGION)] + [side[field, rows, :]]

    def from_west(row):
        turned = [rolled(value, 1, 1) for value in row]
        return [jnp.where(first_lane, turned[c - 1], turned[c]) for c in range(COLS)]

    def from_east(row):
        turned = [rolled(value, -1, 1) for value in row]
        return [jnp.where(last_lane, turned[(c + 1) % COLS], turned[c]) for c in range(COLS)]

    def join(f, *rows):
        return [f(*values) for values in zip(*rows)]

    def down(row):
        return [rolled(value, 1, 0) for value in row]

    def up(row):
        return [rolled(value, -1, 0) for value in row]

    def load(ref, k):
        return [ref[k, col] for col in range(COLS)]

    def store(ref, k, row):
        for col in range(COLS):
            ref[k, col] = row[col]

    def corner_depth(above, here):
        both = join(jnp.minimum, above, here)
        return join(jnp.minimum, both, from_west(both))

    def gathered(row):
        return join(jnp.add, row, from_east(row))

    above = down(strided(masked_ref, 0, CHUNK - 1))
    for k in range(CHUNK):
        here = strided(masked_ref, 0, k)
        store(corner, k, corner_depth(above, here))
        above = here
    for k in range(CHUNK):
        under = load(corner, k + 1) if k + 1 < CHUNK else up(load(corner, 0))
        around = gathered(join(jnp.add, load(corner, k), under))
        source, masked = strided(source_ref, 1, k), strided(masked_ref, 0, k)
        for col in range(COLS):
            inv = 1.0 / (surface_term + 0.75 * around[col])
            start = inv * jnp.where(masked[col] > 0.0, source[col], 0.0)
            inverse[k, col] = 0.25 * inv
            diagonal[k, col] = inv * (surface_term + around[col])
            residual[k, col] = start
            direction[k, col] = opening * start
            total[k, col] = opening * start

    def sweep(index, final):
        carry_scale, forward_scale = scale_ref[index, 0], scale_ref[index, 1]
        above = down(load(direction, CHUNK - 1))
        for k in range(CHUNK):
            here = load(direction, k)
            both = join(jnp.add, above, here)
            spread = join(jnp.add, both, from_west(both))
            store(flow, k, join(jnp.multiply, spread, load(corner, k)))
            above = here
        for k in range(CHUNK):
            under = load(flow, k + 1) if k + 1 < CHUNK else up(load(flow, 0))
            back = gathered(join(jnp.add, load(flow, k), under))
            for col in range(REGION if final else COLS):
                here = direction[k, col]
                rest = residual[k, col] - diagonal[k, col] * here + inverse[k, col] * back[col]
                turned = carry_scale * here + forward_scale * rest
                summed = total[k, col] + turned
                if final:
                    standard[col, pl.ds(k, 8, stride=CHUNK), :] = summed
                else:
                    residual[k, col] = rest
                    direction[k, col] = turned
                    total[k, col] = summed

    lax.fori_loop(0, ITERS - 2, lambda index, _: sweep(index, False), None)
    sweep(ITERS - 2, True)

    for extra in range(MOVE):
        block_of(myself, (myself + 127) % 128, KEPT + extra, owner_ref, standard, one_ref, extra)
        block_of(myself, (myself + 126) % 128, KEPT + extra, owner_ref, standard, two_ref, extra)


def block_of(myself, sender, slot, owner_ref, standard, ref, index):
    region, row, col = place(owner_ref[sender * SLOTS + slot])
    first = pl.multiple_of(row * ROWS, ROWS)
    value = standard[col, pl.ds(first, ROWS), :]
    ref[index] = jnp.where(region == myself, value, 0.0)


def write_kernel(owner_ref, standard, out_ref, tail_ref):
    myself = lax.axis_index("bx") * 8 + lax.axis_index("by")
    for slot in range(SLOTS):
        block_of(myself, myself, slot, owner_ref, standard, out_ref, slot)
    for extra in range(MOVE):
        tail_ref[extra] = out_ref[KEPT + extra]


def tail_kernel(heights_ref, tail_ref, one_ref, two_ref, out_ref, joined, sem):
    del heights_ref
    joined[...] = tail_ref[...] + (one_ref[...] + two_ref[...])
    copy = pltpu.make_async_copy(joined, out_ref.at[pl.ds(KEPT, MOVE)], sem)
    copy.start()
    copy.wait()


def whole(space=VMEM):
    return pl.BlockSpec(memory_space=space)


def ring(value, steps):
    count = lax.axis_size("bx") * lax.axis_size("by")
    return lax.ppermute(value, ("bx", "by"), [(i, (i + steps) % count) for i in range(count)])


def along(value, axis, steps):
    count = lax.axis_size(axis)
    return lax.ppermute(value, axis, [(i, (i + steps) % count) for i in range(count)])


def near(value):
    return pltpu.with_memory_space_constraint(value, VMEM)


def distant(value):
    return pltpu.with_memory_space_constraint(value, HBM)


def on_device(tendency, thickness, depth, block_owner, block_mask, ocean_counts):
    f32 = jnp.float32
    params = pltpu.CompilerParams(vmem_limit_bytes=32 << 20)
    far = pl.BlockSpec(memory_space=HBM)

    def here(*dims):
        return pltpu.VMEM(dims, f32)

    field = (REGION, PACK_ROWS, LANES)
    moved, bottom, upper, lower, source, masked = pl.pallas_call(
        forcing_kernel,
        in_specs=[far] * 6,
        out_specs=[whole()] * 6,
        out_shape=[
            here(MOVE, ROWS, LANES),
            here(MOVE, 16, LANES),
            here(32, REGION * LANES),
            here(32, REGION * LANES),
            here(*field),
            here(*field),
        ],
        scratch_shapes=[
            pltpu.SMEM(thickness.shape, f32),
            pltpu.SMEM(block_owner.shape, jnp.int32),
            pltpu.SMEM(ocean_counts.shape, jnp.int32),
            pltpu.SMEM(block_mask.shape, jnp.int32),
            pltpu.VMEM((SLOTS, LEVELS, ROWS, LANES), jnp.bfloat16),
            pltpu.VMEM((OWN_ROWS, REGION * LANES), f32),
            pltpu.SemaphoreType.DMA((4,)),
            pltpu.SemaphoreType.DMA((SLOTS,)),
            pltpu.SemaphoreType.DMA,
        ],
        compiler_params=params,
        name="forcing",
    )(*map(distant, (thickness, block_owner, ocean_counts, block_mask, tendency, depth)))
    one, two, three = ring(moved, 1), ring(moved, 2), ring(bottom, 3)
    north = along(lower, "by", 1)
    south = along(upper, "by", -1)

    inputs = [near(x) for x in (source, masked, moved, one, two, three, north, south)]
    source, masked, left, right = pl.pallas_call(
        gather_kernel,
        in_specs=[whole(SMEM)] + [whole()] * 8,
        out_specs=[whole()] * 4,
        out_shape=[here(*field), here(*field), here(FOLD, LANES), here(FOLD, LANES)],
        input_output_aliases={1: 0, 2: 1},
        compiler_params=params,
        name="assemble",
    )(block_owner, *inputs)
    west = along(right, "bx", 1)
    east = along(left, "bx", -1)

    scales = jnp.asarray(chebyshev_plan()[1], f32)
    inputs = [near(x) for x in (source, masked, west, east)]
    heights, first, second = pl.pallas_call(
        solve_kernel,
        in_specs=[whole(SMEM)] * 2 + [whole()] * 4,
        out_specs=[whole()] * 3,
        out_shape=[
            here(REGION, EXT_ROWS, LANES),
            here(MOVE, ROWS, LANES),
            here(MOVE, ROWS, LANES),
        ],
        scratch_shapes=[pltpu.VMEM((2, PACK_ROWS, LANES), f32)]
        + [pltpu.VMEM((CHUNK, COLS, 8, LANES), f32)] * 7,
        compiler_params=params,
        name="solve",
    )(block_owner, scales, *inputs)
    back = ring(first, -1), ring(second, -2)

    out, tail = pl.pallas_call(
        write_kernel,
        in_specs=[whole(SMEM), whole()],
        out_specs=[whole()] * 2,
        out_shape=[jax.ShapeDtypeStruct((SLOTS, ROWS, LANES), f32), here(MOVE, ROWS, LANES)],
        compiler_params=params,
        name="write",
    )(block_owner, near(heights))
    return pl.pallas_call(
        tail_kernel,
        in_specs=[far] + [whole()] * 3,
        out_specs=far,
        out_shape=jax.ShapeDtypeStruct((SLOTS, ROWS, LANES), f32),
        input_output_aliases={0: 0},
        scratch_shapes=[here(MOVE, ROWS, LANES), pltpu.SemaphoreType.DMA],
        compiler_params=params,
        name="tail",
    )(out, near(tail), near(back[0]), near(back[1]))


def solution(mesh):
    placed = (
        P(("bx", "by"), None, None, None),
        P(),
        P("by", "bx"),
        P(),
        P("by", "bx"),
        P("by", "bx"),
    )
    return jax.shard_map(
        on_device,
        mesh=mesh,
        in_specs=placed,
        out_specs=P(("bx", "by"), None, None),
        check_vma=False,
    )
```

```python
import jax
import jax.numpy as jnp
from jax import lax
from jax.experimental import pallas as pl
from jax.experimental.pallas import tpu as pltpu
from jax.sharding import PartitionSpec as P

MOVE = 2
ITERS = 10
ROWS, LANES = 64, 128
SLOTS = 12
KEPT = SLOTS - MOVE
LEVELS = 40
REGION = 4
OWN_ROWS = REGION * ROWS
CHUNK = 35
EXT_ROWS = 8 * CHUNK
FOLD = 72
PACK_ROWS = 4 * FOLD
COLS = REGION + 1

surface_term = 0.1
lower_bound = 0.05
upper_bound = 2.0

VMEM = pltpu.MemorySpace.VMEM
SMEM = pltpu.MemorySpace.SMEM
HBM = pltpu.MemorySpace.HBM


def chebyshev_plan():
    centre_value = (upper_bound + lower_bound) / 2.0
    half_width = (upper_bound - lower_bound) / 2.0
    ratio_value = centre_value / half_width
    weight = 1.0 / ratio_value
    scales = []
    for sweep in range(ITERS):
        renewed = 1.0 / (2.0 * ratio_value - weight)
        scales.append((renewed * weight, 2.0 * renewed / half_width))
        weight = renewed
    return (1.0 / centre_value, scales)


def place(block):
    row, col = block // 64, block % 64
    return (col // REGION) * 8 + row // REGION, row % REGION, col % REGION


def rolled(value, steps, axis):
    return pltpu.roll(value, steps % value.shape[axis], axis)


def wetness(rows, count, mask):
    position = lax.broadcasted_iota(jnp.int32, (rows, LANES), 0) * LANES + (
        lax.broadcasted_iota(jnp.int32, (rows, LANES), 1)
    )
    return (position < count) & (mask == 1)


def forcing_kernel(
    thick_in, owner_in, count_in, mask_in, tend_ref, depth_ref,
    inner_ref, outer_ref, moved_ref, bottom_ref, source_ref, masked_ref,
    thick_ref, owner_ref, count_ref, mask_ref, pair, levels, sea, table_sem, level_sem, sea_sem,
):
    myself = lax.axis_index("bx") * 8 + lax.axis_index("by")
    tables = []
    for index, (table_in, table_ref) in enumerate(
        ((count_in, count_ref), (mask_in, mask_ref), (thick_in, thick_ref), (owner_in, owner_ref))
    ):
        copy = pltpu.make_async_copy(table_in, table_ref, table_sem.at[index])
        copy.start()
        tables.append(copy)
    sea_copy = pltpu.make_async_copy(depth_ref, sea, sea_sem)
    sea_copy.start()
    copies = []
    for slot in range(SLOTS):
        copy = pltpu.make_async_copy(tend_ref.at[slot], levels.at[slot], level_sem.at[slot])
        copy.start()
        copies.append(copy)

    odd = lax.axis_index("by") % 2
    ahead_ref, back_ref = pair.at[odd], pair.at[1 - odd]
    ahead_ref[4:8, 16:32, :] = jnp.zeros((REGION, 16, LANES), jnp.float32)
    back_ref[...] = jnp.zeros((8, 32, LANES), jnp.float32)
    source_ref[...] = jnp.zeros(source_ref.shape, jnp.float32)
    for copy in tables:
        copy.wait()
    sea_copy.wait()
    for col in range(REGION):
        lanes = slice(col * LANES, (col + 1) * LANES)
        for row in range(REGION):
            rows = slice(row * ROWS, (row + 1) * ROWS)
            wet = wetness(ROWS, count_ref[row, col], mask_ref[row, col])
            value = jnp.where(wet, sea[rows, lanes], 0.0)
            masked_ref[col, rows, :] = value
            if row == 0:
                back_ref[4 + col, 0:16, :] = value[0:16, :]
            if row == REGION - 1:
                ahead_ref[4 + col, 0:16, :] = value[48:64, :]
        masked_ref[col, OWN_ROWS:PACK_ROWS, :] = jnp.zeros((PACK_ROWS - OWN_ROWS, LANES), jnp.float32)

    for slot in range(SLOTS):
        copies[slot].wait()
        totals = [jnp.zeros((16, LANES), jnp.float32) for _ in range(ROWS // 16)]
        for level in range(LEVELS):
            weight = thick_ref[level]
            for tile in range(ROWS // 16):
                part = levels[slot, level, tile * 16 : tile * 16 + 16, :].astype(jnp.float32)
                totals[tile] = totals[tile] + part * weight
        if slot >= KEPT:
            for tile, value in enumerate(totals):
                moved_ref[slot - KEPT, tile * 16 : tile * 16 + 16, :] = value
                half = slice(tile % 2 * 16, tile % 2 * 16 + 16)
                ahead_ref[(slot - KEPT) * 2 + tile // 2, half, :] = value
            bottom_ref[slot - KEPT] = totals[-1]
        region, row, col = place(owner_ref[myself * SLOTS + slot])

        @pl.when(region == myself)
        def _():
            for tile, value in enumerate(totals):
                first = pl.multiple_of(row * ROWS + tile * 16, 16)
                source_ref[col, pl.ds(first, 16), :] = value

        @pl.when((region == myself) & (row == 0))
        def _():
            back_ref[4 + col, 16:32, :] = totals[0]

        @pl.when((region == myself) & (row == REGION - 1))
        def _():
            ahead_ref[4 + col, 16:32, :] = totals[-1]

    inner_ref[...] = pair[0]
    outer_ref[...] = pair[1]


def gather_kernel(
    owner_ref, source_in, masked_in, moved_ref, inner_ref, outer_ref, two_ref, three_ref,
    source_ref, masked_ref, inner_side_ref, outer_side_ref,
    pair,
):
    del source_in, masked_in
    pair[0] = inner_ref[...]
    pair[1] = outer_ref[...]
    odd = lax.axis_index("by") % 2
    one_ref, under_ref = pair.at[1 - odd], pair.at[odd]
    row_index = lax.axis_index("by")
    myself = lax.axis_index("bx") * 8 + row_index
    end = OWN_ROWS + 8
    lane = lax.broadcasted_iota(jnp.int32, (8, LANES), 1)
    upper = lax.broadcasted_iota(jnp.int32, (8, LANES), 0) < 4

    not_south = row_index == 7
    not_north = row_index == 0
    for col in range(REGION):
        south_ref = under_ref.at[4 + col]
        south = [jnp.where(not_south, 0.0, south_ref[8 * i : 8 * i + 8, :]) for i in range(2)]
        north_ref = one_ref.at[4 + col]
        north = [jnp.where(not_north, 0.0, north_ref[8 * i : 8 * i + 8, :]) for i in range(2)]
        masked_ref[col, OWN_ROWS:end, :] = south[0]
        masked_ref[col, end : end + 8, :] = jnp.where(upper, south[1], north[0])
        masked_ref[col, end + 8 : end + 16, :] = north[1]
        source_ref[col, OWN_ROWS:end, :] = south_ref[16:24, :]
        source_ref[col, end : end + 8, :] = jnp.where(
            upper, south_ref[24:32, :], north_ref[16:24, :]
        )
        source_ref[col, end + 8 : end + 16, :] = north_ref[24:32, :]

    def spread(sender, slot, block, bottom, inside=True, above=True, below=True):
        region, row, col = place(owner_ref[sender * SLOTS + slot])
        if inside:

            @pl.when(region == myself)
            def _():
                first = pl.multiple_of(row * ROWS, ROWS)
                source_ref[col, pl.ds(first, ROWS), :] = block[...].reshape(ROWS, LANES)

        if below:

            @pl.when((region == myself + 1) & (row == 0))
            def _():
                source_ref[col, OWN_ROWS:end, :] = block[0, 0:8, :]
                mixed = source_ref[col, end : end + 8, :]
                source_ref[col, end : end + 8, :] = jnp.where(upper, block[0, 8:16, :], mixed)

        if above:

            @pl.when((region == myself - 1) & (row == REGION - 1))
            def _():
                mixed = source_ref[col, end : end + 8, :]
                source_ref[col, end : end + 8, :] = jnp.where(upper, mixed, bottom[0:8, :])
                source_ref[col, end + 8 : end + 16, :] = bottom[8:16, :]

    for extra in range(MOVE):
        slot = KEPT + extra
        block = moved_ref.at[extra : extra + 1]
        spread(myself, slot, block, None, inside=False, above=False)
        block = one_ref.at[2 * extra : 2 * extra + 2]
        spread((myself + 127) % 128, slot, block, None, above=False)
        block = two_ref.at[extra : extra + 1]
        spread((myself + 126) % 128, slot, block, block.at[0, 48:64, :], below=False)
        spread((myself + 125) % 128, slot, None, three_ref.at[extra], inside=False, below=False)

    even = lax.axis_index("bx") % 2 == 0
    for row in range(FOLD // 8):
        left = jnp.zeros((8, LANES), jnp.float32)
        right = jnp.zeros((8, LANES), jnp.float32)
        for group in range(4):
            rows = slice(group * FOLD + row * 8, group * FOLD + row * 8 + 8)
            for field, ref in enumerate((masked_ref, source_ref)):
                to = 32 * group + 16 * field
                here = (lane >= to) & (lane < to + 16)
                left = jnp.where(here, rolled(ref[0, rows, :], to, 1), left)
                right = jnp.where(here, rolled(ref[REGION - 1, rows, :], to + 16, 1), right)
        inner_side_ref[row * 8 : row * 8 + 8, :] = jnp.where(even, right, left)
        outer_side_ref[row * 8 : row * 8 + 8, :] = jnp.where(even, left, right)


class Sweeper:
    def __init__(self, cols, scale_ref, fields):
        self.cols, self.scale_ref = cols, scale_ref
        self.direction, self.residual, self.total = fields[:3]
        self.corner, self.inverse, self.diagonal, self.flow = fields[3:]
        lane = lax.broadcasted_iota(jnp.int32, (8, LANES), 1)
        self.first_lane, self.last_lane = lane == 0, lane == LANES - 1

    def from_west(self, row):
        turned = [rolled(value, 1, 1) for value in row]
        if self.cols == 1:
            return turned
        return [jnp.where(self.first_lane, turned[c - 1], turned[c]) for c in range(self.cols)]

    def gathered(self, row):
        turned = [rolled(value, -1, 1) for value in row]
        if self.cols > 1:
            following = turned[1:] + turned[:1]
            turned = join(lambda a, b: jnp.where(self.last_lane, a, b), following, turned)
        return join(jnp.add, row, turned)

    def load(self, ref, k):
        return [ref[k, col] for col in range(self.cols)]

    def store(self, ref, k, row):
        for col in range(self.cols):
            ref[k, col] = row[col]

    def prepare(self, masked_ref, source_ref):
        def strided(ref, k):
            return [ref[col, pl.ds(k, 8, stride=CHUNK), :] for col in range(self.cols)]

        opening, _ = chebyshev_plan()
        above = turn(strided(masked_ref, CHUNK - 1), 1)
        for k in range(CHUNK):
            here = strided(masked_ref, k)
            both = join(jnp.minimum, above, here)
            self.store(self.corner, k, join(jnp.minimum, both, self.from_west(both)))
            above = here
        for k in range(CHUNK):
            around = self.gathered(join(jnp.add, self.load(self.corner, k), self.below(self.corner, k)))
            source, masked = strided(source_ref, k), strided(masked_ref, k)
            for col in range(self.cols):
                inv = 1.0 / (surface_term + 0.75 * around[col])
                start = inv * jnp.where(masked[col] > 0.0, source[col], 0.0)
                self.inverse[k, col] = 0.25 * inv
                self.diagonal[k, col] = inv * (surface_term + around[col])
                self.residual[k, col] = start
                self.direction[k, col] = opening * start
                self.total[k, col] = opening * start

    def below(self, ref, k):
        return self.load(ref, k + 1) if k + 1 < CHUNK else turn(self.load(ref, 0), -1)

    def sweep(self, index, final=None):
        carry_scale, forward_scale = self.scale_ref[index, 0], self.scale_ref[index, 1]
        above = turn(self.load(self.direction, CHUNK - 1), 1)
        for k in range(CHUNK):
            here = self.load(self.direction, k)
            both = join(jnp.add, above, here)
            spread = join(jnp.add, both, self.from_west(both))
            self.store(self.flow, k, join(jnp.multiply, spread, self.load(self.corner, k)))
            above = here
        for k in range(CHUNK):
            back = self.gathered(join(jnp.add, self.load(self.flow, k), self.below(self.flow, k)))
            for col in range(self.cols):
                here = self.direction[k, col]
                rest = self.residual[k, col] - self.diagonal[k, col] * here
                rest = rest + self.inverse[k, col] * back[col]
                turned = carry_scale * here + forward_scale * rest
                summed = self.total[k, col] + turned
                if final is not None:
                    final(k, col, summed)
                else:
                    self.residual[k, col] = rest
                    self.direction[k, col] = turned
                    self.total[k, col] = summed

    def solve(self, final):
        lax.fori_loop(0, ITERS - 2, lambda index, _: self.sweep(index), None)
        self.sweep(ITERS - 2, final)


def join(f, *rows):
    return [f(*values) for values in zip(*rows)]


def turn(row, steps):
    return [rolled(value, steps, 0) for value in row]


def region_kernel(scale_ref, source_ref, masked_ref, standard, *fields):
    sweeper = Sweeper(REGION, scale_ref, fields)
    sweeper.prepare(masked_ref, source_ref)

    def final(k, col, value):
        standard[col, pl.ds(k, 8, stride=CHUNK), :] = value

    sweeper.solve(final)


def sides_kernel(
    owner_ref, scale_ref, standard_in, source_ref, masked_ref, inner_ref, outer_ref,
    standard, one_ref, two_ref,
    depth_side, source_side, *fields,
):
    del standard_in
    myself = lax.axis_index("bx") * 8 + lax.axis_index("by")
    lane = lax.broadcasted_iota(jnp.int32, (8, LANES), 1)
    even = lax.axis_index("bx") % 2 == 0
    outer_west, outer_east = lane < 16, (lane >= 96) & (lane < 112)
    own_west, own_east = (lane >= 16) & (lane < 48), (lane >= 64) & (lane < 96)
    for row in range(FOLD // 8):
        rows = slice(row * 8, row * 8 + 8)
        inner, outer = inner_ref[rows, :], outer_ref[rows, :]
        west, east = jnp.where(even, outer, inner), jnp.where(even, inner, outer)
        for group in range(4):
            first = group * FOLD + row * 8
            for field, (ref, side) in enumerate(((masked_ref, depth_side), (source_ref, source_side))):
                start = 32 * group + 16 * field
                inside = rolled(ref[0, first : first + 8, :], 16, 1)
                value = jnp.where(own_west, inside, 0.0)
                inside = rolled(ref[REGION - 1, first : first + 8, :], -32, 1)
                value = jnp.where(own_east, inside, value)
                value = jnp.where(outer_west, rolled(west, -start, 1), value)
                value = jnp.where(outer_east, rolled(east, 96 - start, 1), value)
                side[0, first : first + 8, :] = value

    sweeper = Sweeper(1, scale_ref, fields)
    sweeper.prepare(depth_side, source_side)
    first_columns, last_columns = lane < 16, lane >= 112

    def final(k, col, value):
        rows = pl.ds(k, 8, stride=CHUNK)
        standard[0, rows, :] = jnp.where(first_columns, rolled(value, -16, 1), standard[0, rows, :])
        last = REGION - 1
        standard[last, rows, :] = jnp.where(last_columns, rolled(value, 32, 1), standard[last, rows, :])

    sweeper.solve(final)
    for extra in range(MOVE):
        block_of(myself, (myself + 127) % 128, KEPT + extra, owner_ref, standard, one_ref, extra)
        block_of(myself, (myself + 126) % 128, KEPT + extra, owner_ref, standard, two_ref, extra)


def block_of(myself, sender, slot, owner_ref, standard, ref, index):
    region, row, col = place(owner_ref[sender * SLOTS + slot])
    first = pl.multiple_of(row * ROWS, ROWS)
    value = standard[col, pl.ds(first, ROWS), :]
    ref[index] = jnp.where(region == myself, value, 0.0)


def write_kernel(owner_ref, standard, out_ref, tail_ref):
    myself = lax.axis_index("bx") * 8 + lax.axis_index("by")
    for slot in range(SLOTS):
        block_of(myself, myself, slot, owner_ref, standard, out_ref, slot)
    for extra in range(MOVE):
        tail_ref[extra] = out_ref[KEPT + extra]


def tail_kernel(heights_ref, tail_ref, one_ref, two_ref, out_ref, joined, sem):
    del heights_ref
    joined[...] = tail_ref[...] + (one_ref[...] + two_ref[...])
    copy = pltpu.make_async_copy(joined, out_ref.at[pl.ds(KEPT, MOVE)], sem)
    copy.start()
    copy.wait()


def whole(space=VMEM):
    return pl.BlockSpec(memory_space=space)


def ring(value, steps, senders=range(8)):
    count = lax.axis_size("bx") * lax.axis_size("by")
    pairs = [(i, (i + steps) % count) for i in range(count) if i % 8 in senders]
    return lax.ppermute(value, ("bx", "by"), pairs)


def inner_swap(value, axis):
    return lax.ppermute(value, axis, [(i, i ^ 1) for i in range(lax.axis_size(axis))])


def outer_swap(value, axis):
    count = lax.axis_size(axis)
    pairs = [(i, (i + 1 if i % 2 else i - 1) % count) for i in range(count)]
    return lax.ppermute(value, axis, pairs)


def outer_ring_swap(value):
    count = lax.axis_size("bx") * lax.axis_size("by")
    pairs = [(i, (i + 1) % count) for i in range(1, count, 2)]
    pairs += [(i, i - 1) for i in range(0, count, 2) if i % 8]
    return lax.ppermute(value, ("bx", "by"), pairs)


def near(value):
    return pltpu.with_memory_space_constraint(value, VMEM)


def distant(value):
    return pltpu.with_memory_space_constraint(value, HBM)


def on_device(tendency, thickness, depth, block_owner, block_mask, ocean_counts):
    f32 = jnp.float32
    params = pltpu.CompilerParams(vmem_limit_bytes=32 << 20)
    far = pl.BlockSpec(memory_space=HBM)

    def here(*dims):
        return pltpu.VMEM(dims, f32)

    field = (REGION, PACK_ROWS, LANES)
    inner, outer, moved, bottom, source, masked = pl.pallas_call(
        forcing_kernel,
        in_specs=[far] * 6,
        out_specs=[whole()] * 6,
        out_shape=[
            here(8, 32, LANES),
            here(8, 32, LANES),
            here(MOVE, ROWS, LANES),
            here(MOVE, 16, LANES),
            here(*field),
            here(*field),
        ],
        scratch_shapes=[
            pltpu.SMEM(thickness.shape, f32),
            pltpu.SMEM(block_owner.shape, jnp.int32),
            pltpu.SMEM(ocean_counts.shape, jnp.int32),
            pltpu.SMEM(block_mask.shape, jnp.int32),
            here(2, 8, 32, LANES),
            pltpu.VMEM((SLOTS, LEVELS, ROWS, LANES), jnp.bfloat16),
            pltpu.VMEM((OWN_ROWS, REGION * LANES), f32),
            pltpu.SemaphoreType.DMA((4,)),
            pltpu.SemaphoreType.DMA((SLOTS,)),
            pltpu.SemaphoreType.DMA,
        ],
        compiler_params=params,
        name="forcing",
    )(*map(distant, (thickness, block_owner, ocean_counts, block_mask, tendency, depth)))
    outer = outer_ring_swap(outer)
    two = ring(moved, 2)
    three = ring(bottom, 3, (0, 1, 2, 3, 4, 6, 7))
    inner = inner_swap(inner, "by")

    inputs = [near(x) for x in (source, masked, moved, inner, outer, two, three)]
    source, masked, inner, outer = pl.pallas_call(
        gather_kernel,
        in_specs=[whole(SMEM)] + [whole()] * 7,
        out_specs=[whole()] * 4,
        out_shape=[here(*field), here(*field), here(FOLD, LANES), here(FOLD, LANES)],
        input_output_aliases={1: 0, 2: 1},
        scratch_shapes=[here(2, 8, 32, LANES)],
        compiler_params=params,
        name="assemble",
    )(block_owner, *inputs)
    inner, outer = inner_swap(inner, "bx"), outer_swap(outer, "bx")

    scales = jnp.asarray(chebyshev_plan()[1], f32)
    heights = pl.pallas_call(
        region_kernel,
        in_specs=[whole(SMEM)] + [whole()] * 2,
        out_specs=whole(),
        out_shape=here(REGION, EXT_ROWS, LANES),
        scratch_shapes=[here(CHUNK, REGION, 8, LANES)] * 7,
        compiler_params=params,
        name="region",
    )(scales, near(source), near(masked))

    inputs = [near(x) for x in (heights, source, masked, inner, outer)]
    heights, first, second = pl.pallas_call(
        sides_kernel,
        in_specs=[whole(SMEM)] * 2 + [whole()] * 5,
        out_specs=[whole()] * 3,
        out_shape=[
            here(REGION, EXT_ROWS, LANES),
            here(MOVE, ROWS, LANES),
            here(MOVE, ROWS, LANES),
        ],
        input_output_aliases={2: 0},
        scratch_shapes=[here(1, PACK_ROWS, LANES)] * 2 + [here(CHUNK, 1, 8, LANES)] * 7,
        compiler_params=params,
        name="sides",
    )(block_owner, scales, *inputs)
    back = ring(first, -1), ring(second, -2)

    out, tail = pl.pallas_call(
        write_kernel,
        in_specs=[whole(SMEM), whole()],
        out_specs=[whole()] * 2,
        out_shape=[jax.ShapeDtypeStruct((SLOTS, ROWS, LANES), f32), here(MOVE, ROWS, LANES)],
        compiler_params=params,
        name="write",
    )(block_owner, near(heights))
    return pl.pallas_call(
        tail_kernel,
        in_specs=[far] + [whole()] * 3,
        out_specs=far,
        out_shape=jax.ShapeDtypeStruct((SLOTS, ROWS, LANES), f32),
        input_output_aliases={0: 0},
        scratch_shapes=[here(MOVE, ROWS, LANES), pltpu.SemaphoreType.DMA],
        compiler_params=params,
        name="tail",
    )(out, near(tail), near(back[0]), near(back[1]))


def solution(mesh):
    placed = (
        P(("bx", "by"), None, None, None),
        P(),
        P("by", "bx"),
        P(),
        P("by", "bx"),
        P("by", "bx"),
    )
    return jax.shard_map(
        on_device,
        mesh=mesh,
        in_specs=placed,
        out_specs=P(("bx", "by"), None, None),
        check_vma=False,
    )
```

```python
import jax
import jax.numpy as jnp
from jax import lax
from jax.experimental import pallas as pl
from jax.experimental.pallas import tpu as pltpu
from jax.sharding import PartitionSpec as P

MOVE = 2
ITERS = 10
ROWS, LANES = 64, 128
SLOTS = 12
KEPT = SLOTS - MOVE
LEVELS = 40
REGION = 4
OWN_ROWS = REGION * ROWS
CHUNK = 35
EXT_ROWS = 8 * CHUNK
FOLD = 72
PACK_ROWS = 4 * FOLD
COLS = REGION + 1

surface_term = 0.1
lower_bound = 0.05
upper_bound = 2.0

VMEM = pltpu.MemorySpace.VMEM
SMEM = pltpu.MemorySpace.SMEM
HBM = pltpu.MemorySpace.HBM


def chebyshev_plan():
    centre_value = (upper_bound + lower_bound) / 2.0
    half_width = (upper_bound - lower_bound) / 2.0
    ratio_value = centre_value / half_width
    weight = 1.0 / ratio_value
    scales = []
    for sweep in range(ITERS):
        renewed = 1.0 / (2.0 * ratio_value - weight)
        scales.append((renewed * weight, 2.0 * renewed / half_width))
        weight = renewed
    return (1.0 / centre_value, scales)


def place(block):
    row, col = block // 64, block % 64
    return (col // REGION) * 8 + row // REGION, row % REGION, col % REGION


def rolled(value, steps, axis):
    return pltpu.roll(value, steps % value.shape[axis], axis)


def wetness(rows, count, mask):
    position = lax.broadcasted_iota(jnp.int32, (rows, LANES), 0) * LANES + (
        lax.broadcasted_iota(jnp.int32, (rows, LANES), 1)
    )
    return (position < count) & (mask == 1)


def level_sum(tend_ref, slot, thick_ref):
    totals = [jnp.zeros((16, LANES), jnp.float32) for _ in range(ROWS // 16)]
    for level in range(LEVELS):
        weight = thick_ref[level]
        for tile in range(ROWS // 16):
            part = tend_ref[slot, level, tile * 16 : tile * 16 + 16, :].astype(jnp.float32)
            totals[tile] = totals[tile] + part * weight
    return totals


def moved_kernel(
    thick_in, count_in, mask_in, tend_ref, depth_ref,
    moved_ref, masked_ref,
    thick_ref, count_ref, mask_ref, levels, sea, table_sem, level_sem, sea_sem,
):
    tables = []
    for index, (table_in, table_ref) in enumerate(
        ((thick_in, thick_ref), (count_in, count_ref), (mask_in, mask_ref))
    ):
        copy = pltpu.make_async_copy(table_in, table_ref, table_sem.at[index])
        copy.start()
        tables.append(copy)
    copies = []
    for extra in range(MOVE):
        copy = pltpu.make_async_copy(
            tend_ref.at[KEPT + extra], levels.at[extra], level_sem.at[extra]
        )
        copy.start()
        copies.append(copy)
    sea_copy = pltpu.make_async_copy(depth_ref, sea, sea_sem)
    sea_copy.start()
    for copy in tables:
        copy.wait()
    for extra in range(MOVE):
        copies[extra].wait()
        totals = level_sum(levels, extra, thick_ref)
        for tile, value in enumerate(totals):
            moved_ref[extra, tile * 16 : tile * 16 + 16, :] = value
    sea_copy.wait()
    for col in range(REGION):
        lanes = slice(col * LANES, (col + 1) * LANES)
        for row in range(REGION):
            rows = slice(row * ROWS, (row + 1) * ROWS)
            wet = wetness(ROWS, count_ref[row, col], mask_ref[row, col])
            masked_ref[col, rows, :] = jnp.where(wet, sea[rows, lanes], 0.0)
        masked_ref[col, OWN_ROWS:PACK_ROWS, :] = jnp.zeros((PACK_ROWS - OWN_ROWS, LANES), jnp.float32)


def forcing_kernel(
    thick_in, owner_in, tend_ref, masked_ref, moved_ref,
    inner_ref, outer_ref, source_ref,
    thick_ref, owner_ref, pair, table_sem,
):
    tables = []
    for index, (table_in, table_ref) in enumerate(((thick_in, thick_ref), (owner_in, owner_ref))):
        copy = pltpu.make_async_copy(table_in, table_ref, table_sem.at[index])
        copy.start()
        tables.append(copy)
    myself = lax.axis_index("bx") * 8 + lax.axis_index("by")
    upper = lax.broadcasted_iota(jnp.int32, (8, LANES), 0) < 4
    odd = lax.axis_index("by") % 2
    ahead_ref, back_ref = pair.at[odd], pair.at[1 - odd]
    source_ref[...] = jnp.zeros(source_ref.shape, jnp.float32)
    for copy in tables:
        copy.wait()

    def put(slot, totals):
        region, row, col = place(owner_ref[myself * SLOTS + slot])

        @pl.when(region == myself)
        def _():
            for tile, value in enumerate(totals):
                first = pl.multiple_of(row * ROWS + tile * 16, 16)
                source_ref[col, pl.ds(first, 16), :] = value

    for slot in range(KEPT):
        put(slot, level_sum(tend_ref, slot, thick_ref))
    for extra in range(MOVE):
        put(KEPT + extra, [moved_ref[extra, 16 * tile : 16 * tile + 16, :] for tile in range(4)])

    for col in range(REGION):
        back_ref[col, 0:8, :] = masked_ref[col, 0:8, :]
        back_ref[col, 8:16, :] = source_ref[col, 0:8, :]
        back_ref[col, 16:24, :] = jnp.where(
            upper, masked_ref[col, 8:16, :], rolled(source_ref[col, 8:16, :], 4, 0)
        )
        last = OWN_ROWS - 8
        ahead_ref[col, 0:8, :] = masked_ref[col, last:OWN_ROWS, :]
        ahead_ref[col, 8:16, :] = source_ref[col, last:OWN_ROWS, :]
        ahead_ref[col, 16:24, :] = jnp.where(
            upper, rolled(source_ref[col, last - 8 : last, :], 4, 0), masked_ref[col, last - 8 : last, :]
        )
    inner_ref[...] = pair[0]
    outer_ref[...] = pair[1]


def gather_kernel(
    owner_ref, source_in, masked_in, moved_ref, inner_ref, outer_ref, mixed_ref, two_ref, passed_two_ref,
    source_ref, masked_ref, inner_side_ref, outer_side_ref,
    pair, held,
):
    del source_in, masked_in
    pair[0] = inner_ref[...]
    pair[1] = outer_ref[...]
    odd = lax.axis_index("by") % 2
    over_ref, under_ref = pair.at[1 - odd], pair.at[odd]
    held[0] = mixed_ref[...]
    held[1] = passed_two_ref[...]
    one_ref, three_ref = held.at[1 - odd], held.at[odd]
    row_index = lax.axis_index("by")
    myself = lax.axis_index("bx") * 8 + row_index
    end = OWN_ROWS + 8
    lane = lax.broadcasted_iota(jnp.int32, (8, LANES), 1)
    upper = lax.broadcasted_iota(jnp.int32, (8, LANES), 0) < 4

    not_south = row_index == 7
    not_north = row_index == 0
    for col in range(REGION):
        def take(ref, missing):
            depth = [jnp.where(missing, 0.0, ref[col, rows, :]) for rows in (slice(0, 8), slice(16, 24))]
            return depth, [ref[col, 8:16, :], rolled(ref[col, 16:24, :], 4, 0)]

        south, below = take(under_ref, not_south)
        north, above = take(over_ref, not_north)
        masked_ref[col, OWN_ROWS:end, :] = south[0]
        masked_ref[col, end : end + 8, :] = jnp.where(upper, south[1], north[1])
        masked_ref[col, end + 8 : end + 16, :] = north[0]
        source_ref[col, OWN_ROWS:end, :] = below[0]
        source_ref[col, end : end + 8, :] = jnp.where(upper, below[1], above[1])
        source_ref[col, end + 8 : end + 16, :] = above[0]

    def spread(sender, slot, block, bottom, inside=True, above=True, below=True):
        region, row, col = place(owner_ref[sender * SLOTS + slot])
        if inside:

            @pl.when(region == myself)
            def _():
                first = pl.multiple_of(row * ROWS, ROWS)
                source_ref[col, pl.ds(first, ROWS), :] = block[...]

        if below:

            @pl.when((region == myself + 1) & (row == 0))
            def _():
                source_ref[col, OWN_ROWS:end, :] = block[0:8, :]
                mixed = source_ref[col, end : end + 8, :]
                source_ref[col, end : end + 8, :] = jnp.where(upper, block[8:16, :], mixed)

        if above:

            @pl.when((region == myself - 1) & (row == REGION - 1))
            def _():
                mixed = source_ref[col, end : end + 8, :]
                source_ref[col, end : end + 8, :] = jnp.where(upper, mixed, bottom[0:8, :])
                source_ref[col, end + 8 : end + 16, :] = bottom[8:16, :]

    for extra in range(MOVE):
        slot = KEPT + extra
        block = moved_ref.at[extra]
        spread(myself, slot, block, None, inside=False, above=False)
        block = one_ref.at[extra]
        spread((myself + 127) % 128, slot, block, None, above=False)
        block = two_ref.at[extra]
        spread((myself + 126) % 128, slot, block, block.at[48:64, :], below=False)
        spread((myself + 125) % 128, slot, None, three_ref.at[extra, 48:64, :], inside=False, below=False)

    even = lax.axis_index("bx") % 2 == 0
    for row in range(FOLD // 8):
        left = jnp.zeros((8, LANES), jnp.float32)
        right = jnp.zeros((8, LANES), jnp.float32)
        for group in range(4):
            rows = slice(group * FOLD + row * 8, group * FOLD + row * 8 + 8)
            for field, ref in enumerate((masked_ref, source_ref)):
                to = 32 * group + 16 * field
                here = (lane >= to) & (lane < to + 16)
                left = jnp.where(here, rolled(ref[0, rows, :], to, 1), left)
                right = jnp.where(here, rolled(ref[REGION - 1, rows, :], to + 16, 1), right)
        inner_side_ref[row * 8 : row * 8 + 8, :] = jnp.where(even, right, left)
        outer_side_ref[row * 8 : row * 8 + 8, :] = jnp.where(even, left, right)


class Sweeper:
    def __init__(self, cols, scale_ref, fields):
        self.cols, self.scale_ref = cols, scale_ref
        self.direction, self.residual, self.total = fields[:3]
        self.corner, self.inverse, self.diagonal, self.flow = fields[3:]
        lane = lax.broadcasted_iota(jnp.int32, (8, LANES), 1)
        self.first_lane, self.last_lane = lane == 0, lane == LANES - 1

    def from_west(self, row):
        turned = [rolled(value, 1, 1) for value in row]
        if self.cols == 1:
            return turned
        return [jnp.where(self.first_lane, turned[c - 1], turned[c]) for c in range(self.cols)]

    def gathered(self, row):
        turned = [rolled(value, -1, 1) for value in row]
        if self.cols > 1:
            following = turned[1:] + turned[:1]
            turned = join(lambda a, b: jnp.where(self.last_lane, a, b), following, turned)
        return join(jnp.add, row, turned)

    def load(self, ref, k):
        return [ref[k, col] for col in range(self.cols)]

    def store(self, ref, k, row):
        for col in range(self.cols):
            ref[k, col] = row[col]

    def prepare(self, masked_ref, source_ref):
        def strided(ref, k):
            return [ref[col, pl.ds(k, 8, stride=CHUNK), :] for col in range(self.cols)]

        opening, _ = chebyshev_plan()
        above = turn(strided(masked_ref, CHUNK - 1), 1)
        for k in range(CHUNK):
            here = strided(masked_ref, k)
            both = join(jnp.minimum, above, here)
            self.store(self.corner, k, join(jnp.minimum, both, self.from_west(both)))
            above = here
        for k in range(CHUNK):
            around = self.gathered(join(jnp.add, self.load(self.corner, k), self.below(self.corner, k)))
            source, masked = strided(source_ref, k), strided(masked_ref, k)
            for col in range(self.cols):
                inv = 1.0 / (surface_term + 0.75 * around[col])
                start = inv * jnp.where(masked[col] > 0.0, source[col], 0.0)
                self.inverse[k, col] = 0.25 * inv
                self.diagonal[k, col] = inv * (surface_term + around[col])
                self.residual[k, col] = start
                self.direction[k, col] = opening * start

    def below(self, ref, k):
        return self.load(ref, k + 1) if k + 1 < CHUNK else turn(self.load(ref, 0), -1)

    def sweep(self, index, add, final=None):
        carry_scale, forward_scale = self.scale_ref[index, 0], self.scale_ref[index, 1]
        above = turn(self.load(self.direction, CHUNK - 1), 1)
        for k in range(CHUNK):
            here = self.load(self.direction, k)
            both = join(jnp.add, above, here)
            spread = join(jnp.add, both, self.from_west(both))
            self.store(self.flow, k, join(jnp.multiply, spread, self.load(self.corner, k)))
            above = here
        for k in range(CHUNK):
            back = self.gathered(join(jnp.add, self.load(self.flow, k), self.below(self.flow, k)))
            for col in range(self.cols):
                here = self.direction[k, col]
                rest = self.residual[k, col] - self.diagonal[k, col] * here
                rest = rest + self.inverse[k, col] * back[col]
                turned = carry_scale * here + forward_scale * rest
                if add == "first":
                    self.total[k, col] = here + turned
                elif final is not None:
                    final(k, col, self.total[k, col] + (here + turned))
                elif add:
                    self.total[k, col] = self.total[k, col] + (here + turned)
                if final is None:
                    self.residual[k, col] = rest
                    self.direction[k, col] = turned

    def solve(self, final):
        self.sweep(0, "first")

        def two_sweeps(pair, _):
            self.sweep(2 * pair + 1, False)
            self.sweep(2 * pair + 2, True)

        lax.fori_loop(0, ITERS // 2 - 2, two_sweeps, None, unroll=self.cols == 1)
        self.sweep(ITERS - 3, False)
        self.sweep(ITERS - 2, True, final)


def join(f, *rows):
    return [f(*values) for values in zip(*rows)]


def turn(row, steps):
    return [rolled(value, steps, 0) for value in row]


def region_kernel(scale_ref, source_ref, masked_ref, standard, *fields):
    sweeper = Sweeper(REGION, scale_ref, fields)
    sweeper.prepare(masked_ref, source_ref)

    def final(k, col, value):
        standard[col, pl.ds(k, 8, stride=CHUNK), :] = value

    sweeper.solve(final)


def sides_kernel(
    owner_ref, scale_ref, standard_in, source_ref, masked_ref, inner_ref, outer_ref,
    standard, one_ref, two_ref,
    depth_side, source_side, *fields,
):
    del standard_in
    myself = lax.axis_index("bx") * 8 + lax.axis_index("by")
    lane = lax.broadcasted_iota(jnp.int32, (8, LANES), 1)
    even = lax.axis_index("bx") % 2 == 0
    outer_west, outer_east = lane < 16, (lane >= 96) & (lane < 112)
    own_west, own_east = (lane >= 16) & (lane < 48), (lane >= 64) & (lane < 96)
    for row in range(FOLD // 8):
        rows = slice(row * 8, row * 8 + 8)
        inner, outer = inner_ref[rows, :], outer_ref[rows, :]
        west, east = jnp.where(even, outer, inner), jnp.where(even, inner, outer)
        for group in range(4):
            first = group * FOLD + row * 8
            for field, (ref, side) in enumerate(((masked_ref, depth_side), (source_ref, source_side))):
                start = 32 * group + 16 * field
                inside = rolled(ref[0, first : first + 8, :], 16, 1)
                value = jnp.where(own_west, inside, 0.0)
                inside = rolled(ref[REGION - 1, first : first + 8, :], -32, 1)
                value = jnp.where(own_east, inside, value)
                value = jnp.where(outer_west, rolled(west, -start, 1), value)
                value = jnp.where(outer_east, rolled(east, 96 - start, 1), value)
                side[0, first : first + 8, :] = value

    sweeper = Sweeper(1, scale_ref, fields)
    sweeper.prepare(depth_side, source_side)
    first_columns, last_columns = lane < 16, lane >= 112

    def final(k, col, value):
        rows = pl.ds(k, 8, stride=CHUNK)
        standard[0, rows, :] = jnp.where(first_columns, rolled(value, -16, 1), standard[0, rows, :])
        last = REGION - 1
        standard[last, rows, :] = jnp.where(last_columns, rolled(value, 32, 1), standard[last, rows, :])

    sweeper.solve(final)
    for extra in range(MOVE):
        block_of(myself, (myself + 127) % 128, KEPT + extra, owner_ref, standard, one_ref, extra)
        block_of(myself, (myself + 126) % 128, KEPT + extra, owner_ref, standard, two_ref, extra)


def block_of(myself, sender, slot, owner_ref, standard, ref, index):
    region, row, col = place(owner_ref[sender * SLOTS + slot])
    first = pl.multiple_of(row * ROWS, ROWS)
    value = standard[col, pl.ds(first, ROWS), :]
    ref[index] = jnp.where(region == myself, value, 0.0)


def write_kernel(owner_ref, standard, out_ref, tail_ref):
    myself = lax.axis_index("bx") * 8 + lax.axis_index("by")
    for slot in range(SLOTS):
        block_of(myself, myself, slot, owner_ref, standard, out_ref, slot)
    for extra in range(MOVE):
        tail_ref[extra] = out_ref[KEPT + extra]


def tail_kernel(heights_ref, tail_ref, passed_ref, back_ref, out_ref, joined, sem):
    del heights_ref
    even = lax.axis_index("by") % 2 == 0
    joined[...] = tail_ref[...] + (jnp.where(even, passed_ref[...], 0.0) + back_ref[...])
    copy = pltpu.make_async_copy(joined, out_ref.at[pl.ds(KEPT, MOVE)], sem)
    copy.start()
    copy.wait()


def whole(space=VMEM):
    return pl.BlockSpec(memory_space=space)


def ring(value, steps):
    count = lax.axis_size("bx") * lax.axis_size("by")
    return lax.ppermute(value, ("bx", "by"), [(i, (i + steps) % count) for i in range(count)])


def inner_swap(value, axis):
    return lax.ppermute(value, axis, [(i, i ^ 1) for i in range(lax.axis_size(axis))])


def outer_swap(value, axis):
    count = lax.axis_size(axis)
    pairs = [(i, (i + 1 if i % 2 else i - 1) % count) for i in range(count)]
    return lax.ppermute(value, axis, pairs)


def outer_row_swap(value):
    rows, count = lax.axis_size("by"), lax.axis_size("bx") * lax.axis_size("by")
    pairs = []
    for i in range(count):
        row, col = i % rows, i // rows
        if row in (0, rows - 1):
            pairs.append((i, (col ^ 1) * rows + row))
        else:
            pairs.append((i, i + 1 if row % 2 else i - 1))
    return lax.ppermute(value, ("bx", "by"), pairs)


def mixed_ring(value):
    count = lax.axis_size("bx") * lax.axis_size("by")
    pairs = [(i, (i + (3 if i % 2 else 1)) % count) for i in range(count)]
    pairs = [(i, i - 5 if i % 8 == 5 else j) for i, j in pairs]
    return lax.ppermute(value, ("bx", "by"), pairs)


def near(value):
    return pltpu.with_memory_space_constraint(value, VMEM)


def distant(value):
    return pltpu.with_memory_space_constraint(value, HBM)


def on_device(tendency, thickness, depth, block_owner, block_mask, ocean_counts):
    f32 = jnp.float32
    params = pltpu.CompilerParams(vmem_limit_bytes=16 << 20)
    far = pl.BlockSpec(memory_space=HBM)

    def here(*dims):
        return pltpu.VMEM(dims, f32)

    field = (REGION, PACK_ROWS, LANES)
    tables = [distant(x) for x in (thickness, ocean_counts, block_mask)]
    moved, masked = pl.pallas_call(
        moved_kernel,
        in_specs=[far] * 5,
        out_specs=[whole()] * 2,
        out_shape=[here(MOVE, ROWS, LANES), here(*field)],
        scratch_shapes=[
            pltpu.SMEM(thickness.shape, f32),
            pltpu.SMEM(ocean_counts.shape, jnp.int32),
            pltpu.SMEM(block_mask.shape, jnp.int32),
            pltpu.VMEM((MOVE, LEVELS, ROWS, LANES), jnp.bfloat16),
            here(OWN_ROWS, REGION * LANES),
            pltpu.SemaphoreType.DMA((3,)),
            pltpu.SemaphoreType.DMA((MOVE,)),
            pltpu.SemaphoreType.DMA,
        ],
        compiler_params=params,
        name="moved",
    )(*tables, distant(tendency), distant(depth))
    two = ring(moved, 2)
    mixed = mixed_ring(moved)
    inner, outer, source = pl.pallas_call(
        forcing_kernel,
        in_specs=[far] * 2 + [whole()] * 3,
        out_specs=[whole()] * 3,
        out_shape=[here(REGION, 24, LANES), here(REGION, 24, LANES), here(*field)],
        scratch_shapes=[
            pltpu.SMEM(thickness.shape, f32),
            pltpu.SMEM(block_owner.shape, jnp.int32),
            here(2, REGION, 24, LANES),
            pltpu.SemaphoreType.DMA((2,)),
        ],
        compiler_params=params,
        name="forcing",
    )(distant(thickness), distant(block_owner), near(tendency), near(masked), near(moved))
    late_two, _ = lax.optimization_barrier((two, inner))
    outer = outer_row_swap(outer)
    inner = inner_swap(inner, "by")
    passed_two = inner_swap(late_two, "by")

    inputs = [near(x) for x in (source, masked, moved, inner, outer, mixed, two, passed_two)]
    source, masked, inner, outer = pl.pallas_call(
        gather_kernel,
        in_specs=[whole(SMEM)] + [whole()] * 8,
        out_specs=[whole()] * 4,
        out_shape=[here(*field), here(*field), here(FOLD, LANES), here(FOLD, LANES)],
        input_output_aliases={1: 0, 2: 1},
        scratch_shapes=[here(2, REGION, 24, LANES), here(2, MOVE, ROWS, LANES)],
        compiler_params=params,
        name="assemble",
    )(block_owner, *inputs)
    inner, outer = inner_swap(inner, "bx"), outer_swap(outer, "bx")

    scales = jnp.asarray(chebyshev_plan()[1], f32)
    heights = pl.pallas_call(
        region_kernel,
        in_specs=[whole(SMEM)] + [whole()] * 2,
        out_specs=whole(),
        out_shape=here(REGION, EXT_ROWS, LANES),
        scratch_shapes=[here(CHUNK, REGION, 8, LANES)] * 7,
        compiler_params=params,
        name="region",
    )(scales, near(source), near(masked))

    inputs = [near(x) for x in (heights, source, masked, inner, outer)]
    heights, first, second = pl.pallas_call(
        sides_kernel,
        in_specs=[whole(SMEM)] * 2 + [whole()] * 5,
        out_specs=[whole()] * 3,
        out_shape=[
            here(REGION, EXT_ROWS, LANES),
            here(MOVE, ROWS, LANES),
            here(MOVE, ROWS, LANES),
        ],
        input_output_aliases={2: 0},
        scratch_shapes=[here(1, PACK_ROWS, LANES)] * 2 + [here(CHUNK, 1, 8, LANES)] * 7,
        compiler_params=params,
        name="sides",
    )(block_owner, scales, *inputs)
    passed = inner_swap(first, "by")
    odd = lax.axis_index("by") % 2 == 1
    back = ring(jnp.where(odd, second + passed, second), -2)

    out, tail = pl.pallas_call(
        write_kernel,
        in_specs=[whole(SMEM), whole()],
        out_specs=[whole()] * 2,
        out_shape=[jax.ShapeDtypeStruct((SLOTS, ROWS, LANES), f32), here(MOVE, ROWS, LANES)],
        compiler_params=params,
        name="write",
    )(block_owner, near(heights))
    return pl.pallas_call(
        tail_kernel,
        in_specs=[far] + [whole()] * 3,
        out_specs=far,
        out_shape=jax.ShapeDtypeStruct((SLOTS, ROWS, LANES), f32),
        input_output_aliases={0: 0},
        scratch_shapes=[here(MOVE, ROWS, LANES), pltpu.SemaphoreType.DMA],
        compiler_params=params,
        name="tail",
    )(out, near(tail), near(passed), near(back))


def solution(mesh):
    placed = (
        P(("bx", "by"), None, None, None),
        P(),
        P("by", "bx"),
        P(),
        P("by", "bx"),
        P("by", "bx"),
    )
    return jax.shard_map(
        on_device,
        mesh=mesh,
        in_specs=placed,
        out_specs=P(("bx", "by"), None, None),
        check_vma=False,
    )
```

```python
import jax
import jax.numpy as jnp
from jax import lax
from jax.experimental import pallas as pl
from jax.experimental.pallas import tpu as pltpu
from jax.sharding import PartitionSpec as P

MOVE = 2
ITERS = 10
ROWS, LANES = 64, 128
SLOTS = 12
KEPT = SLOTS - MOVE
LEVELS = 40
REGION = 4
OWN_ROWS = REGION * ROWS
CHUNK = 35
EXT_ROWS = 8 * CHUNK
FOLD = 72
PACK_ROWS = 4 * FOLD
COLS = REGION + 1

surface_term = 0.1
lower_bound = 0.05
upper_bound = 2.0

VMEM = pltpu.MemorySpace.VMEM
SMEM = pltpu.MemorySpace.SMEM
HBM = pltpu.MemorySpace.HBM


def chebyshev_plan():
    centre_value = (upper_bound + lower_bound) / 2.0
    half_width = (upper_bound - lower_bound) / 2.0
    ratio_value = centre_value / half_width
    weight = 1.0 / ratio_value
    scales = []
    for sweep in range(ITERS):
        renewed = 1.0 / (2.0 * ratio_value - weight)
        scales.append((renewed * weight, 2.0 * renewed / half_width))
        weight = renewed
    return (1.0 / centre_value, scales)


def place(block):
    row, col = block // 64, block % 64
    return (col // REGION) * 8 + row // REGION, row % REGION, col % REGION


def rolled(value, steps, axis):
    return pltpu.roll(value, steps % value.shape[axis], axis)


def wetness(rows, count, mask):
    position = lax.broadcasted_iota(jnp.int32, (rows, LANES), 0) * LANES + (
        lax.broadcasted_iota(jnp.int32, (rows, LANES), 1)
    )
    return (position < count) & (mask == 1)


def level_sum(tend_ref, slot, thick_ref):
    totals = [jnp.zeros((16, LANES), jnp.float32) for _ in range(ROWS // 16)]
    for level in range(LEVELS):
        weight = thick_ref[level]
        for tile in range(ROWS // 16):
            part = tend_ref[slot, level, tile * 16 : tile * 16 + 16, :].astype(jnp.float32)
            totals[tile] = totals[tile] + part * weight
    return totals


def moved_kernel(
    thick_in, tend_ref,
    moved_ref,
    thick_ref, levels, table_sem, level_sem,
):
    table = pltpu.make_async_copy(thick_in, thick_ref, table_sem)
    table.start()
    copies = []
    for extra in range(MOVE):
        copy = pltpu.make_async_copy(
            tend_ref.at[KEPT + extra], levels.at[extra], level_sem.at[extra]
        )
        copy.start()
        copies.append(copy)
    table.wait()
    for extra in range(MOVE):
        copies[extra].wait()
        totals = level_sum(levels, extra, thick_ref)
        for tile, value in enumerate(totals):
            moved_ref[extra, tile * 16 : tile * 16 + 16, :] = value


def forcing_kernel(
    thick_in, owner_in, count_in, mask_in, tend_ref, depth_ref, moved_ref,
    inner_ref, outer_ref, source_ref, masked_ref,
    thick_ref, owner_ref, count_ref, mask_ref, sea, pair, table_sem, sea_sem,
):
    sea_copy = pltpu.make_async_copy(depth_ref, sea, sea_sem)
    tables = []
    for index, (table_in, table_ref) in enumerate(
        ((thick_in, thick_ref), (owner_in, owner_ref), (count_in, count_ref), (mask_in, mask_ref))
    ):
        copy = pltpu.make_async_copy(table_in, table_ref, table_sem.at[index])
        copy.start()
        tables.append(copy)
    myself = lax.axis_index("bx") * 8 + lax.axis_index("by")
    upper = lax.broadcasted_iota(jnp.int32, (8, LANES), 0) < 4
    odd = lax.axis_index("by") % 2
    ahead_ref, back_ref = pair.at[odd], pair.at[1 - odd]
    source_ref[...] = jnp.zeros(source_ref.shape, jnp.float32)
    sea_copy.start()
    for copy in tables:
        copy.wait()

    def put(slot, totals):
        region, row, col = place(owner_ref[myself * SLOTS + slot])

        @pl.when(region == myself)
        def _():
            for tile, value in enumerate(totals):
                first = pl.multiple_of(row * ROWS + tile * 16, 16)
                source_ref[col, pl.ds(first, 16), :] = value

    for slot in range(KEPT):
        put(slot, level_sum(tend_ref, slot, thick_ref))
    for extra in range(MOVE):
        put(KEPT + extra, [moved_ref[extra, 16 * tile : 16 * tile + 16, :] for tile in range(4)])

    sea_copy.wait()
    for col in range(REGION):
        lanes = slice(col * LANES, (col + 1) * LANES)
        for row in range(REGION):
            rows = slice(row * ROWS, (row + 1) * ROWS)
            wet = wetness(ROWS, count_ref[row, col], mask_ref[row, col])
            masked_ref[col, rows, :] = jnp.where(wet, sea[rows, lanes], 0.0)
        masked_ref[col, OWN_ROWS:PACK_ROWS, :] = jnp.zeros((PACK_ROWS - OWN_ROWS, LANES), jnp.float32)

    for col in range(REGION):
        back_ref[col, 0:8, :] = masked_ref[col, 0:8, :]
        back_ref[col, 8:16, :] = source_ref[col, 0:8, :]
        back_ref[col, 16:24, :] = jnp.where(
            upper, masked_ref[col, 8:16, :], rolled(source_ref[col, 8:16, :], 4, 0)
        )
        last = OWN_ROWS - 8
        ahead_ref[col, 0:8, :] = masked_ref[col, last:OWN_ROWS, :]
        ahead_ref[col, 8:16, :] = source_ref[col, last:OWN_ROWS, :]
        ahead_ref[col, 16:24, :] = jnp.where(
            upper, rolled(source_ref[col, last - 8 : last, :], 4, 0), masked_ref[col, last - 8 : last, :]
        )
    inner_ref[...] = pair[0]
    outer_ref[...] = pair[1]


def gather_kernel(
    owner_ref, source_in, masked_in, moved_ref, inner_ref, outer_ref, mixed_ref, two_ref, passed_two_ref,
    source_ref, masked_ref, inner_side_ref, outer_side_ref,
    pair, held,
):
    del source_in, masked_in
    pair[0] = inner_ref[...]
    pair[1] = outer_ref[...]
    odd = lax.axis_index("by") % 2
    over_ref, under_ref = pair.at[1 - odd], pair.at[odd]
    held[0] = mixed_ref[...]
    held[1] = passed_two_ref[...]
    one_ref, three_ref = held.at[1 - odd], held.at[odd]
    row_index = lax.axis_index("by")
    myself = lax.axis_index("bx") * 8 + row_index
    end = OWN_ROWS + 8
    lane = lax.broadcasted_iota(jnp.int32, (8, LANES), 1)
    upper = lax.broadcasted_iota(jnp.int32, (8, LANES), 0) < 4

    not_south = row_index == 7
    not_north = row_index == 0
    for col in range(REGION):
        def take(ref, missing):
            depth = [jnp.where(missing, 0.0, ref[col, rows, :]) for rows in (slice(0, 8), slice(16, 24))]
            return depth, [ref[col, 8:16, :], rolled(ref[col, 16:24, :], 4, 0)]

        south, below = take(under_ref, not_south)
        north, above = take(over_ref, not_north)
        masked_ref[col, OWN_ROWS:end, :] = south[0]
        masked_ref[col, end : end + 8, :] = jnp.where(upper, south[1], north[1])
        masked_ref[col, end + 8 : end + 16, :] = north[0]
        source_ref[col, OWN_ROWS:end, :] = below[0]
        source_ref[col, end : end + 8, :] = jnp.where(upper, below[1], above[1])
        source_ref[col, end + 8 : end + 16, :] = above[0]

    def spread(sender, slot, block, bottom, inside=True, above=True, below=True):
        region, row, col = place(owner_ref[sender * SLOTS + slot])
        if inside:

            @pl.when(region == myself)
            def _():
                first = pl.multiple_of(row * ROWS, ROWS)
                source_ref[col, pl.ds(first, ROWS), :] = block[...]

        if below:

            @pl.when((region == myself + 1) & (row == 0))
            def _():
                source_ref[col, OWN_ROWS:end, :] = block[0:8, :]
                mixed = source_ref[col, end : end + 8, :]
                source_ref[col, end : end + 8, :] = jnp.where(upper, block[8:16, :], mixed)

        if above:

            @pl.when((region == myself - 1) & (row == REGION - 1))
            def _():
                mixed = source_ref[col, end : end + 8, :]
                source_ref[col, end : end + 8, :] = jnp.where(upper, mixed, bottom[0:8, :])
                source_ref[col, end + 8 : end + 16, :] = bottom[8:16, :]

    for extra in range(MOVE):
        slot = KEPT + extra
        block = moved_ref.at[extra]
        spread(myself, slot, block, None, inside=False, above=False)
        block = one_ref.at[extra]
        spread((myself + 127) % 128, slot, block, None, above=False)
        block = two_ref.at[extra]
        spread((myself + 126) % 128, slot, block, block.at[48:64, :], below=False)
        spread((myself + 125) % 128, slot, None, three_ref.at[extra, 48:64, :], inside=False, below=False)

    even = lax.axis_index("bx") % 2 == 0
    for row in range(FOLD // 8):
        left = jnp.zeros((8, LANES), jnp.float32)
        right = jnp.zeros((8, LANES), jnp.float32)
        for group in range(4):
            rows = slice(group * FOLD + row * 8, group * FOLD + row * 8 + 8)
            for field, ref in enumerate((masked_ref, source_ref)):
                to = 32 * group + 16 * field
                here = (lane >= to) & (lane < to + 16)
                left = jnp.where(here, rolled(ref[0, rows, :], to, 1), left)
                right = jnp.where(here, rolled(ref[REGION - 1, rows, :], to + 16, 1), right)
        inner_side_ref[row * 8 : row * 8 + 8, :] = jnp.where(even, right, left)
        outer_side_ref[row * 8 : row * 8 + 8, :] = jnp.where(even, left, right)


class Sweeper:
    def __init__(self, cols, scale_ref, fields):
        self.cols, self.scale_ref = cols, scale_ref
        self.direction, self.residual, self.total = fields[:3]
        self.corner, self.inverse, self.diagonal, self.flow = fields[3:]
        lane = lax.broadcasted_iota(jnp.int32, (8, LANES), 1)
        self.first_lane, self.last_lane = lane == 0, lane == LANES - 1

    def from_west(self, row):
        turned = [rolled(value, 1, 1) for value in row]
        if self.cols == 1:
            return turned
        return [jnp.where(self.first_lane, turned[c - 1], turned[c]) for c in range(self.cols)]

    def gathered(self, row):
        turned = [rolled(value, -1, 1) for value in row]
        if self.cols > 1:
            following = turned[1:] + turned[:1]
            turned = join(lambda a, b: jnp.where(self.last_lane, a, b), following, turned)
        return join(jnp.add, row, turned)

    def load(self, ref, k):
        return [ref[k, col] for col in range(self.cols)]

    def store(self, ref, k, row):
        for col in range(self.cols):
            ref[k, col] = row[col]

    def prepare(self, masked_ref, source_ref):
        def strided(ref, k):
            return [ref[col, pl.ds(k, 8, stride=CHUNK), :] for col in range(self.cols)]

        opening, _ = chebyshev_plan()
        above = turn(strided(masked_ref, CHUNK - 1), 1)
        for k in range(CHUNK):
            here = strided(masked_ref, k)
            both = join(jnp.minimum, above, here)
            self.store(self.corner, k, join(jnp.minimum, both, self.from_west(both)))
            above = here
        for k in range(CHUNK):
            around = self.gathered(join(jnp.add, self.load(self.corner, k), self.below(self.corner, k)))
            source, masked = strided(source_ref, k), strided(masked_ref, k)
            for col in range(self.cols):
                inv = 1.0 / (surface_term + 0.75 * around[col])
                start = inv * jnp.where(masked[col] > 0.0, source[col], 0.0)
                self.inverse[k, col] = 0.25 * inv
                self.diagonal[k, col] = inv * (surface_term + around[col])
                self.residual[k, col] = start
                self.direction[k, col] = opening * start

    def below(self, ref, k):
        return self.load(ref, k + 1) if k + 1 < CHUNK else turn(self.load(ref, 0), -1)

    def sweep(self, index, add, final=None):
        carry_scale, forward_scale = self.scale_ref[index, 0], self.scale_ref[index, 1]
        above = turn(self.load(self.direction, CHUNK - 1), 1)
        for k in range(CHUNK):
            here = self.load(self.direction, k)
            both = join(jnp.add, above, here)
            spread = join(jnp.add, both, self.from_west(both))
            self.store(self.flow, k, join(jnp.multiply, spread, self.load(self.corner, k)))
            above = here
        for k in range(CHUNK):
            back = self.gathered(join(jnp.add, self.load(self.flow, k), self.below(self.flow, k)))
            for col in range(self.cols):
                here = self.direction[k, col]
                rest = self.residual[k, col] - self.diagonal[k, col] * here
                rest = rest + self.inverse[k, col] * back[col]
                turned = carry_scale * here + forward_scale * rest
                if add == "first":
                    self.total[k, col] = here + turned
                elif final is not None:
                    final(k, col, self.total[k, col] + (here + turned))
                elif add:
                    self.total[k, col] = self.total[k, col] + (here + turned)
                if final is None:
                    self.residual[k, col] = rest
                    self.direction[k, col] = turned

    def solve(self, final):
        self.sweep(0, "first")

        def two_sweeps(pair, _):
            self.sweep(2 * pair + 1, False)
            self.sweep(2 * pair + 2, True)

        lax.fori_loop(0, ITERS // 2 - 2, two_sweeps, None, unroll=self.cols == 1)
        self.sweep(ITERS - 3, False)
        self.sweep(ITERS - 2, True, final)


def join(f, *rows):
    return [f(*values) for values in zip(*rows)]


def turn(row, steps):
    return [rolled(value, steps, 0) for value in row]


def region_kernel(scale_ref, source_ref, masked_ref, standard, *fields):
    sweeper = Sweeper(REGION, scale_ref, fields)
    sweeper.prepare(masked_ref, source_ref)

    def final(k, col, value):
        standard[col, pl.ds(k, 8, stride=CHUNK), :] = value

    sweeper.solve(final)


def sides_kernel(
    owner_ref, scale_ref, standard_in, source_ref, masked_ref, inner_ref, outer_ref,
    standard, one_ref, two_ref,
    depth_side, source_side, *fields,
):
    del standard_in
    myself = lax.axis_index("bx") * 8 + lax.axis_index("by")
    lane = lax.broadcasted_iota(jnp.int32, (8, LANES), 1)
    even = lax.axis_index("bx") % 2 == 0
    outer_west, outer_east = lane < 16, (lane >= 96) & (lane < 112)
    own_west, own_east = (lane >= 16) & (lane < 48), (lane >= 64) & (lane < 96)
    for row in range(FOLD // 8):
        rows = slice(row * 8, row * 8 + 8)
        inner, outer = inner_ref[rows, :], outer_ref[rows, :]
        west, east = jnp.where(even, outer, inner), jnp.where(even, inner, outer)
        for group in range(4):
            first = group * FOLD + row * 8
            for field, (ref, side) in enumerate(((masked_ref, depth_side), (source_ref, source_side))):
                start = 32 * group + 16 * field
                inside = rolled(ref[0, first : first + 8, :], 16, 1)
                value = jnp.where(own_west, inside, 0.0)
                inside = rolled(ref[REGION - 1, first : first + 8, :], -32, 1)
                value = jnp.where(own_east, inside, value)
                value = jnp.where(outer_west, rolled(west, -start, 1), value)
                value = jnp.where(outer_east, rolled(east, 96 - start, 1), value)
                side[0, first : first + 8, :] = value

    sweeper = Sweeper(1, scale_ref, fields)
    sweeper.prepare(depth_side, source_side)
    first_columns, last_columns = lane < 16, lane >= 112

    def final(k, col, value):
        rows = pl.ds(k, 8, stride=CHUNK)
        standard[0, rows, :] = jnp.where(first_columns, rolled(value, -16, 1), standard[0, rows, :])
        last = REGION - 1
        standard[last, rows, :] = jnp.where(last_columns, rolled(value, 32, 1), standard[last, rows, :])

    sweeper.solve(final)
    for extra in range(MOVE):
        block_of(myself, (myself + 127) % 128, KEPT + extra, owner_ref, standard, one_ref, extra)
        block_of(myself, (myself + 126) % 128, KEPT + extra, owner_ref, standard, two_ref, extra)


def block_of(myself, sender, slot, owner_ref, standard, ref, index):
    region, row, col = place(owner_ref[sender * SLOTS + slot])
    first = pl.multiple_of(row * ROWS, ROWS)
    value = standard[col, pl.ds(first, ROWS), :]
    ref[index] = jnp.where(region == myself, value, 0.0)


def write_kernel(owner_ref, standard, out_ref, tail_ref):
    myself = lax.axis_index("bx") * 8 + lax.axis_index("by")
    for slot in range(SLOTS):
        block_of(myself, myself, slot, owner_ref, standard, out_ref, slot)
    for extra in range(MOVE):
        tail_ref[extra] = out_ref[KEPT + extra]


def tail_kernel(heights_ref, tail_ref, passed_ref, back_ref, out_ref, joined, sem):
    del heights_ref
    even = lax.axis_index("by") % 2 == 0
    joined[...] = tail_ref[...] + (jnp.where(even, passed_ref[...], 0.0) + back_ref[...])
    copy = pltpu.make_async_copy(joined, out_ref.at[pl.ds(KEPT, MOVE)], sem)
    copy.start()
    copy.wait()


def whole(space=VMEM):
    return pl.BlockSpec(memory_space=space)


def ring(value, steps):
    count = lax.axis_size("bx") * lax.axis_size("by")
    return lax.ppermute(value, ("bx", "by"), [(i, (i + steps) % count) for i in range(count)])


def inner_swap(value, axis):
    return lax.ppermute(value, axis, [(i, i ^ 1) for i in range(lax.axis_size(axis))])


def outer_swap(value, axis):
    count = lax.axis_size(axis)
    pairs = [(i, (i + 1 if i % 2 else i - 1) % count) for i in range(count)]
    return lax.ppermute(value, axis, pairs)


def outer_row_swap(value):
    rows, count = lax.axis_size("by"), lax.axis_size("bx") * lax.axis_size("by")
    pairs = []
    for i in range(count):
        row, col = i % rows, i // rows
        if row in (0, rows - 1):
            pairs.append((i, (col ^ 1) * rows + row))
        else:
            pairs.append((i, i + 1 if row % 2 else i - 1))
    return lax.ppermute(value, ("bx", "by"), pairs)


def mixed_ring(value):
    count = lax.axis_size("bx") * lax.axis_size("by")
    pairs = [(i, (i + (3 if i % 2 else 1)) % count) for i in range(count)]
    pairs = [(i, i - 5 if i % 8 == 5 else j) for i, j in pairs]
    return lax.ppermute(value, ("bx", "by"), pairs)


def near(value):
    return pltpu.with_memory_space_constraint(value, VMEM)


def distant(value):
    return pltpu.with_memory_space_constraint(value, HBM)


def on_device(tendency, thickness, depth, block_owner, block_mask, ocean_counts):
    f32 = jnp.float32
    params = pltpu.CompilerParams(vmem_limit_bytes=16 << 20)
    far = pl.BlockSpec(memory_space=HBM)

    def here(*dims):
        return pltpu.VMEM(dims, f32)

    field = (REGION, PACK_ROWS, LANES)
    moved = pl.pallas_call(
        moved_kernel,
        in_specs=[far] * 2,
        out_specs=whole(),
        out_shape=here(MOVE, ROWS, LANES),
        scratch_shapes=[
            pltpu.SMEM(thickness.shape, f32),
            pltpu.VMEM((MOVE, LEVELS, ROWS, LANES), jnp.bfloat16),
            pltpu.SemaphoreType.DMA,
            pltpu.SemaphoreType.DMA((MOVE,)),
        ],
        compiler_params=params,
        name="moved",
    )(distant(thickness), distant(tendency))
    two = ring(moved, 2)
    mixed = mixed_ring(moved)
    inner, outer, source, masked = pl.pallas_call(
        forcing_kernel,
        in_specs=[far] * 4 + [whole(), far, whole()],
        out_specs=[whole()] * 4,
        out_shape=[
            here(REGION, 24, LANES),
            here(REGION, 24, LANES),
            here(*field),
            here(*field),
        ],
        scratch_shapes=[
            pltpu.SMEM(thickness.shape, f32),
            pltpu.SMEM(block_owner.shape, jnp.int32),
            pltpu.SMEM(ocean_counts.shape, jnp.int32),
            pltpu.SMEM(block_mask.shape, jnp.int32),
            here(OWN_ROWS, REGION * LANES),
            here(2, REGION, 24, LANES),
            pltpu.SemaphoreType.DMA((4,)),
            pltpu.SemaphoreType.DMA,
        ],
        compiler_params=params,
        name="forcing",
    )(
        *map(distant, (thickness, block_owner, ocean_counts, block_mask)),
        near(tendency),
        distant(depth),
        near(moved),
    )
    late_two, _ = lax.optimization_barrier((two, inner))
    outer = outer_row_swap(outer)
    inner = inner_swap(inner, "by")
    passed_two = inner_swap(late_two, "by")

    inputs = [near(x) for x in (source, masked, moved, inner, outer, mixed, two, passed_two)]
    source, masked, inner, outer = pl.pallas_call(
        gather_kernel,
        in_specs=[whole(SMEM)] + [whole()] * 8,
        out_specs=[whole()] * 4,
        out_shape=[here(*field), here(*field), here(FOLD, LANES), here(FOLD, LANES)],
        input_output_aliases={1: 0, 2: 1},
        scratch_shapes=[here(2, REGION, 24, LANES), here(2, MOVE, ROWS, LANES)],
        compiler_params=params,
        name="assemble",
    )(block_owner, *inputs)
    inner, outer = inner_swap(inner, "bx"), outer_swap(outer, "bx")

    scales = jnp.asarray(chebyshev_plan()[1], f32)
    heights = pl.pallas_call(
        region_kernel,
        in_specs=[whole(SMEM)] + [whole()] * 2,
        out_specs=whole(),
        out_shape=here(REGION, EXT_ROWS, LANES),
        scratch_shapes=[here(CHUNK, REGION, 8, LANES)] * 7,
        compiler_params=params,
        name="region",
    )(scales, near(source), near(masked))

    inputs = [near(x) for x in (heights, source, masked, inner, outer)]
    heights, first, second = pl.pallas_call(
        sides_kernel,
        in_specs=[whole(SMEM)] * 2 + [whole()] * 5,
        out_specs=[whole()] * 3,
        out_shape=[
            here(REGION, EXT_ROWS, LANES),
            here(MOVE, ROWS, LANES),
            here(MOVE, ROWS, LANES),
        ],
        input_output_aliases={2: 0},
        scratch_shapes=[here(1, PACK_ROWS, LANES)] * 2 + [here(CHUNK, 1, 8, LANES)] * 7,
        compiler_params=params,
        name="sides",
    )(block_owner, scales, *inputs)
    passed = inner_swap(first, "by")
    odd = lax.axis_index("by") % 2 == 1
    back = ring(jnp.where(odd, second + passed, second), -2)

    out, tail = pl.pallas_call(
        write_kernel,
        in_specs=[whole(SMEM), whole()],
        out_specs=[whole()] * 2,
        out_shape=[jax.ShapeDtypeStruct((SLOTS, ROWS, LANES), f32), here(MOVE, ROWS, LANES)],
        compiler_params=params,
        name="write",
    )(block_owner, near(heights))
    return pl.pallas_call(
        tail_kernel,
        in_specs=[far] + [whole()] * 3,
        out_specs=far,
        out_shape=jax.ShapeDtypeStruct((SLOTS, ROWS, LANES), f32),
        input_output_aliases={0: 0},
        scratch_shapes=[here(MOVE, ROWS, LANES), pltpu.SemaphoreType.DMA],
        compiler_params=params,
        name="tail",
    )(out, near(tail), near(passed), near(back))


def solution(mesh):
    placed = (
        P(("bx", "by"), None, None, None),
        P(),
        P("by", "bx"),
        P(),
        P("by", "bx"),
        P("by", "bx"),
    )
    return jax.shard_map(
        on_device,
        mesh=mesh,
        in_specs=placed,
        out_specs=P(("bx", "by"), None, None),
        check_vma=False,
    )
```

```python
import jax
import jax.numpy as jnp
from jax import lax
from jax.experimental import pallas as pl
from jax.experimental.pallas import tpu as pltpu
from jax.sharding import PartitionSpec as P

MOVE = 2
ITERS = 10
ROWS, LANES = 64, 128
SLOTS = 12
KEPT = SLOTS - MOVE
LEVELS = 40
REGION = 4
OWN_ROWS = REGION * ROWS
CHUNK = 35
EXT_ROWS = 8 * CHUNK
FOLD = 72
PACK_ROWS = 4 * FOLD
COLS = REGION + 1

surface_term = 0.1
lower_bound = 0.05
upper_bound = 2.0

VMEM = pltpu.MemorySpace.VMEM
SMEM = pltpu.MemorySpace.SMEM
HBM = pltpu.MemorySpace.HBM


def chebyshev_plan():
    centre_value = (upper_bound + lower_bound) / 2.0
    half_width = (upper_bound - lower_bound) / 2.0
    ratio_value = centre_value / half_width
    weight = 1.0 / ratio_value
    scales = []
    for sweep in range(ITERS):
        renewed = 1.0 / (2.0 * ratio_value - weight)
        scales.append((renewed * weight, 2.0 * renewed / half_width))
        weight = renewed
    return (1.0 / centre_value, scales)


def place(block):
    row, col = block // 64, block % 64
    return (col // REGION) * 8 + row // REGION, row % REGION, col % REGION


def rolled(value, steps, axis):
    return pltpu.roll(value, steps % value.shape[axis], axis)


def wetness(rows, count, mask):
    position = lax.broadcasted_iota(jnp.int32, (rows, LANES), 0) * LANES + (
        lax.broadcasted_iota(jnp.int32, (rows, LANES), 1)
    )
    return (position < count) & (mask == 1)


def level_sum(tend_ref, slot, thick_ref):
    totals = [jnp.zeros((16, LANES), jnp.float32) for _ in range(ROWS // 16)]
    for level in range(LEVELS):
        weight = thick_ref[level]
        for tile in range(ROWS // 16):
            part = tend_ref[slot, level, tile * 16 : tile * 16 + 16, :].astype(jnp.float32)
            totals[tile] = totals[tile] + part * weight
    return totals


def moved_kernel(
    thick_in, tend_ref,
    moved_ref,
    thick_ref, levels, table_sem, level_sem,
):
    table = pltpu.make_async_copy(thick_in, thick_ref, table_sem)
    table.start()
    copies = []
    part = LEVELS // 4
    for extra in range(MOVE):
        for quarter in range(4):
            some = pl.ds(quarter * part, part)
            copy = pltpu.make_async_copy(
                tend_ref.at[KEPT + extra, some], levels.at[extra, some], level_sem.at[extra, quarter]
            )
            copy.start()
            copies.append(copy)
    table.wait()
    for extra in range(MOVE):
        for copy in copies[4 * extra : 4 * extra + 4]:
            copy.wait()
        totals = level_sum(levels, extra, thick_ref)
        for tile, value in enumerate(totals):
            moved_ref[extra, tile * 16 : tile * 16 + 16, :] = value


def forcing_kernel(
    thick_in, owner_in, count_in, mask_in, tend_ref, depth_ref, moved_ref,
    inner_ref, outer_ref, source_ref, masked_ref,
    thick_ref, owner_ref, count_ref, mask_ref, sea, pair, table_sem, sea_sem,
):
    sea_copy = pltpu.make_async_copy(depth_ref, sea, sea_sem)
    tables = []
    for index, (table_in, table_ref) in enumerate(
        ((thick_in, thick_ref), (owner_in, owner_ref), (count_in, count_ref), (mask_in, mask_ref))
    ):
        copy = pltpu.make_async_copy(table_in, table_ref, table_sem.at[index])
        copy.start()
        tables.append(copy)
    myself = lax.axis_index("bx") * 8 + lax.axis_index("by")
    upper = lax.broadcasted_iota(jnp.int32, (8, LANES), 0) < 4
    odd = lax.axis_index("by") % 2
    ahead_ref, back_ref = pair.at[odd], pair.at[1 - odd]
    source_ref[...] = jnp.zeros(source_ref.shape, jnp.float32)
    sea_copy.start()
    for copy in tables:
        copy.wait()

    def put(slot, totals):
        region, row, col = place(owner_ref[myself * SLOTS + slot])

        @pl.when(region == myself)
        def _():
            for tile, value in enumerate(totals):
                first = pl.multiple_of(row * ROWS + tile * 16, 16)
                source_ref[col, pl.ds(first, 16), :] = value

    for slot in range(KEPT):
        put(slot, level_sum(tend_ref, slot, thick_ref))
    for extra in range(MOVE):
        put(KEPT + extra, [moved_ref[extra, 16 * tile : 16 * tile + 16, :] for tile in range(4)])

    sea_copy.wait()
    for col in range(REGION):
        lanes = slice(col * LANES, (col + 1) * LANES)
        for row in range(REGION):
            rows = slice(row * ROWS, (row + 1) * ROWS)
            wet = wetness(ROWS, count_ref[row, col], mask_ref[row, col])
            masked_ref[col, rows, :] = jnp.where(wet, sea[rows, lanes], 0.0)
        masked_ref[col, OWN_ROWS:PACK_ROWS, :] = jnp.zeros((PACK_ROWS - OWN_ROWS, LANES), jnp.float32)

    for col in range(REGION):
        back_ref[col, 0:8, :] = masked_ref[col, 0:8, :]
        back_ref[col, 8:16, :] = source_ref[col, 0:8, :]
        back_ref[col, 16:24, :] = jnp.where(
            upper, masked_ref[col, 8:16, :], rolled(source_ref[col, 8:16, :], 4, 0)
        )
        last = OWN_ROWS - 8
        ahead_ref[col, 0:8, :] = masked_ref[col, last:OWN_ROWS, :]
        ahead_ref[col, 8:16, :] = source_ref[col, last:OWN_ROWS, :]
        ahead_ref[col, 16:24, :] = jnp.where(
            upper, rolled(source_ref[col, last - 8 : last, :], 4, 0), masked_ref[col, last - 8 : last, :]
        )
    inner_ref[...] = pair[0]
    outer_ref[...] = pair[1]


def gather_kernel(
    owner_ref, source_in, masked_in, moved_ref, inner_ref, outer_ref, mixed_ref, two_ref, passed_two_ref,
    source_ref, masked_ref, inner_side_ref, outer_side_ref,
    pair, held,
):
    del source_in, masked_in
    pair[0] = inner_ref[...]
    pair[1] = outer_ref[...]
    odd = lax.axis_index("by") % 2
    over_ref, under_ref = pair.at[1 - odd], pair.at[odd]
    held[0] = mixed_ref[...]
    held[1] = passed_two_ref[...]
    one_ref, three_ref = held.at[1 - odd], held.at[odd]
    row_index = lax.axis_index("by")
    myself = lax.axis_index("bx") * 8 + row_index
    end = OWN_ROWS + 8
    lane = lax.broadcasted_iota(jnp.int32, (8, LANES), 1)
    upper = lax.broadcasted_iota(jnp.int32, (8, LANES), 0) < 4

    not_south = row_index == 7
    not_north = row_index == 0
    for col in range(REGION):
        def take(ref, missing):
            depth = [jnp.where(missing, 0.0, ref[col, rows, :]) for rows in (slice(0, 8), slice(16, 24))]
            return depth, [ref[col, 8:16, :], rolled(ref[col, 16:24, :], 4, 0)]

        south, below = take(under_ref, not_south)
        north, above = take(over_ref, not_north)
        masked_ref[col, OWN_ROWS:end, :] = south[0]
        masked_ref[col, end : end + 8, :] = jnp.where(upper, south[1], north[1])
        masked_ref[col, end + 8 : end + 16, :] = north[0]
        source_ref[col, OWN_ROWS:end, :] = below[0]
        source_ref[col, end : end + 8, :] = jnp.where(upper, below[1], above[1])
        source_ref[col, end + 8 : end + 16, :] = above[0]

    def spread(sender, slot, block, bottom, inside=True, above=True, below=True):
        region, row, col = place(owner_ref[sender * SLOTS + slot])
        if inside:

            @pl.when(region == myself)
            def _():
                first = pl.multiple_of(row * ROWS, ROWS)
                source_ref[col, pl.ds(first, ROWS), :] = block[...]

        if below:

            @pl.when((region == myself + 1) & (row == 0))
            def _():
                source_ref[col, OWN_ROWS:end, :] = block[0:8, :]
                mixed = source_ref[col, end : end + 8, :]
                source_ref[col, end : end + 8, :] = jnp.where(upper, block[8:16, :], mixed)

        if above:

            @pl.when((region == myself - 1) & (row == REGION - 1))
            def _():
                mixed = source_ref[col, end : end + 8, :]
                source_ref[col, end : end + 8, :] = jnp.where(upper, mixed, bottom[0:8, :])
                source_ref[col, end + 8 : end + 16, :] = bottom[8:16, :]

    for extra in range(MOVE):
        slot = KEPT + extra
        block = moved_ref.at[extra]
        spread(myself, slot, block, None, inside=False, above=False)
        block = one_ref.at[extra]
        spread((myself + 127) % 128, slot, block, None, above=False)
        block = two_ref.at[extra]
        spread((myself + 126) % 128, slot, block, block.at[48:64, :], below=False)
        spread((myself + 125) % 128, slot, None, three_ref.at[extra, 48:64, :], inside=False, below=False)

    even = lax.axis_index("bx") % 2 == 0
    for row in range(FOLD // 8):
        left = jnp.zeros((8, LANES), jnp.float32)
        right = jnp.zeros((8, LANES), jnp.float32)
        for group in range(4):
            rows = slice(group * FOLD + row * 8, group * FOLD + row * 8 + 8)
            for field, ref in enumerate((masked_ref, source_ref)):
                to = 32 * group + 16 * field
                here = (lane >= to) & (lane < to + 16)
                left = jnp.where(here, rolled(ref[0, rows, :], to, 1), left)
                right = jnp.where(here, rolled(ref[REGION - 1, rows, :], to + 16, 1), right)
        inner_side_ref[row * 8 : row * 8 + 8, :] = jnp.where(even, right, left)
        outer_side_ref[row * 8 : row * 8 + 8, :] = jnp.where(even, left, right)


class Sweeper:
    def __init__(self, cols, scale_ref, fields):
        self.cols, self.scale_ref = cols, scale_ref
        self.direction, self.residual, self.total = fields[:3]
        self.corner, self.inverse, self.diagonal, self.flow = fields[3:]
        lane = lax.broadcasted_iota(jnp.int32, (8, LANES), 1)
        self.first_lane, self.last_lane = lane == 0, lane == LANES - 1

    def from_west(self, row):
        turned = [rolled(value, 1, 1) for value in row]
        if self.cols == 1:
            return turned
        return [jnp.where(self.first_lane, turned[c - 1], turned[c]) for c in range(self.cols)]

    def gathered(self, row):
        turned = [rolled(value, -1, 1) for value in row]
        if self.cols > 1:
            following = turned[1:] + turned[:1]
            turned = join(lambda a, b: jnp.where(self.last_lane, a, b), following, turned)
        return join(jnp.add, row, turned)

    def load(self, ref, k):
        return [ref[k, col] for col in range(self.cols)]

    def store(self, ref, k, row):
        for col in range(self.cols):
            ref[k, col] = row[col]

    def prepare(self, masked_ref, source_ref):
        def strided(ref, k):
            return [ref[col, pl.ds(k, 8, stride=CHUNK), :] for col in range(self.cols)]

        opening, _ = chebyshev_plan()
        above = turn(strided(masked_ref, CHUNK - 1), 1)
        for k in range(CHUNK):
            here = strided(masked_ref, k)
            both = join(jnp.minimum, above, here)
            self.store(self.corner, k, join(jnp.minimum, both, self.from_west(both)))
            above = here
        for k in range(CHUNK):
            around = self.gathered(join(jnp.add, self.load(self.corner, k), self.below(self.corner, k)))
            source, masked = strided(source_ref, k), strided(masked_ref, k)
            for col in range(self.cols):
                inv = 1.0 / (surface_term + 0.75 * around[col])
                start = inv * jnp.where(masked[col] > 0.0, source[col], 0.0)
                self.inverse[k, col] = 0.25 * inv
                self.diagonal[k, col] = inv * (surface_term + around[col])
                self.residual[k, col] = start
                self.direction[k, col] = opening * start

    def below(self, ref, k):
        return self.load(ref, k + 1) if k + 1 < CHUNK else turn(self.load(ref, 0), -1)

    def sweep(self, index, add, final=None):
        carry_scale, forward_scale = self.scale_ref[index, 0], self.scale_ref[index, 1]
        above = turn(self.load(self.direction, CHUNK - 1), 1)
        for k in range(CHUNK):
            here = self.load(self.direction, k)
            both = join(jnp.add, above, here)
            spread = join(jnp.add, both, self.from_west(both))
            self.store(self.flow, k, join(jnp.multiply, spread, self.load(self.corner, k)))
            above = here
        for k in range(CHUNK):
            back = self.gathered(join(jnp.add, self.load(self.flow, k), self.below(self.flow, k)))
            for col in range(self.cols):
                here = self.direction[k, col]
                rest = self.residual[k, col] - self.diagonal[k, col] * here
                rest = rest + self.inverse[k, col] * back[col]
                turned = carry_scale * here + forward_scale * rest
                if add == "first":
                    self.total[k, col] = here + turned
                elif final is not None:
                    final(k, col, self.total[k, col] + (here + turned))
                elif add:
                    self.total[k, col] = self.total[k, col] + (here + turned)
                if final is None:
                    self.residual[k, col] = rest
                    self.direction[k, col] = turned

    def solve(self, final):
        self.sweep(0, "first")

        def two_sweeps(pair, _):
            self.sweep(2 * pair + 1, False)
            self.sweep(2 * pair + 2, True)

        lax.fori_loop(0, ITERS // 2 - 2, two_sweeps, None, unroll=self.cols == 1)
        self.sweep(ITERS - 3, False)
        self.sweep(ITERS - 2, True, final)


def join(f, *rows):
    return [f(*values) for values in zip(*rows)]


def turn(row, steps):
    return [rolled(value, steps, 0) for value in row]


def region_kernel(scale_ref, source_ref, masked_ref, standard, *fields):
    sweeper = Sweeper(REGION, scale_ref, fields)
    sweeper.prepare(masked_ref, source_ref)

    def final(k, col, value):
        standard[col, pl.ds(k, 8, stride=CHUNK), :] = value

    sweeper.solve(final)


def sides_kernel(
    owner_ref, scale_ref, standard_in, source_ref, masked_ref, inner_ref, outer_ref,
    standard, one_ref, two_ref,
    depth_side, source_side, *fields,
):
    del standard_in
    myself = lax.axis_index("bx") * 8 + lax.axis_index("by")
    lane = lax.broadcasted_iota(jnp.int32, (8, LANES), 1)
    even = lax.axis_index("bx") % 2 == 0
    outer_west, outer_east = lane < 16, (lane >= 96) & (lane < 112)
    own_west, own_east = (lane >= 16) & (lane < 48), (lane >= 64) & (lane < 96)
    for row in range(FOLD // 8):
        rows = slice(row * 8, row * 8 + 8)
        inner, outer = inner_ref[rows, :], outer_ref[rows, :]
        west, east = jnp.where(even, outer, inner), jnp.where(even, inner, outer)
        for group in range(4):
            first = group * FOLD + row * 8
            for field, (ref, side) in enumerate(((masked_ref, depth_side), (source_ref, source_side))):
                start = 32 * group + 16 * field
                inside = rolled(ref[0, first : first + 8, :], 16, 1)
                value = jnp.where(own_west, inside, 0.0)
                inside = rolled(ref[REGION - 1, first : first + 8, :], -32, 1)
                value = jnp.where(own_east, inside, value)
                value = jnp.where(outer_west, rolled(west, -start, 1), value)
                value = jnp.where(outer_east, rolled(east, 96 - start, 1), value)
                side[0, first : first + 8, :] = value

    sweeper = Sweeper(1, scale_ref, fields)
    sweeper.prepare(depth_side, source_side)
    first_columns, last_columns = lane < 16, lane >= 112

    def final(k, col, value):
        rows = pl.ds(k, 8, stride=CHUNK)
        standard[0, rows, :] = jnp.where(first_columns, rolled(value, -16, 1), standard[0, rows, :])
        last = REGION - 1
        standard[last, rows, :] = jnp.where(last_columns, rolled(value, 32, 1), standard[last, rows, :])

    sweeper.solve(final)
    for extra in range(MOVE):
        block_of(myself, (myself + 127) % 128, KEPT + extra, owner_ref, standard, one_ref, extra)
        block_of(myself, (myself + 126) % 128, KEPT + extra, owner_ref, standard, two_ref, extra)


def block_of(myself, sender, slot, owner_ref, standard, ref, index):
    region, row, col = place(owner_ref[sender * SLOTS + slot])
    first = pl.multiple_of(row * ROWS, ROWS)
    value = standard[col, pl.ds(first, ROWS), :]
    ref[index] = jnp.where(region == myself, value, 0.0)


def write_kernel(owner_ref, standard, out_ref, tail_ref):
    myself = lax.axis_index("bx") * 8 + lax.axis_index("by")
    for slot in range(SLOTS):
        block_of(myself, myself, slot, owner_ref, standard, out_ref, slot)
    for extra in range(MOVE):
        tail_ref[extra] = out_ref[KEPT + extra]


def tail_kernel(heights_ref, tail_ref, passed_ref, back_ref, out_ref, joined, sem):
    del heights_ref
    even = lax.axis_index("by") % 2 == 0
    joined[...] = tail_ref[...] + (jnp.where(even, passed_ref[...], 0.0) + back_ref[...])
    copy = pltpu.make_async_copy(joined, out_ref.at[pl.ds(KEPT, MOVE)], sem)
    copy.start()
    copy.wait()


def whole(space=VMEM):
    return pl.BlockSpec(memory_space=space)


def ring(value, steps):
    count = lax.axis_size("bx") * lax.axis_size("by")
    return lax.ppermute(value, ("bx", "by"), [(i, (i + steps) % count) for i in range(count)])


def inner_swap(value, axis):
    return lax.ppermute(value, axis, [(i, i ^ 1) for i in range(lax.axis_size(axis))])


def outer_swap(value, axis):
    count = lax.axis_size(axis)
    pairs = [(i, (i + 1 if i % 2 else i - 1) % count) for i in range(count)]
    return lax.ppermute(value, axis, pairs)


def outer_row_swap(value):
    rows, count = lax.axis_size("by"), lax.axis_size("bx") * lax.axis_size("by")
    pairs = []
    for i in range(count):
        row, col = i % rows, i // rows
        if row in (0, rows - 1):
            pairs.append((i, (col ^ 1) * rows + row))
        else:
            pairs.append((i, i + 1 if row % 2 else i - 1))
    return lax.ppermute(value, ("bx", "by"), pairs)


def mixed_ring(value):
    count = lax.axis_size("bx") * lax.axis_size("by")
    pairs = [(i, (i + (3 if i % 2 else 1)) % count) for i in range(count)]
    pairs = [(i, i - 5 if i % 8 == 5 else j) for i, j in pairs]
    return lax.ppermute(value, ("bx", "by"), pairs)


def near(value):
    return pltpu.with_memory_space_constraint(value, VMEM)


def distant(value):
    return pltpu.with_memory_space_constraint(value, HBM)


def on_device(tendency, thickness, depth, block_owner, block_mask, ocean_counts):
    f32 = jnp.float32
    params = pltpu.CompilerParams(vmem_limit_bytes=16 << 20)
    far = pl.BlockSpec(memory_space=HBM)

    def here(*dims):
        return pltpu.VMEM(dims, f32)

    field = (REGION, PACK_ROWS, LANES)
    moved = pl.pallas_call(
        moved_kernel,
        in_specs=[far] * 2,
        out_specs=whole(),
        out_shape=here(MOVE, ROWS, LANES),
        scratch_shapes=[
            pltpu.SMEM(thickness.shape, f32),
            pltpu.VMEM((MOVE, LEVELS, ROWS, LANES), jnp.bfloat16),
            pltpu.SemaphoreType.DMA,
            pltpu.SemaphoreType.DMA((MOVE, 4)),
        ],
        compiler_params=params,
        name="moved",
    )(distant(thickness), distant(tendency))
    two = ring(moved, 2)
    mixed = mixed_ring(moved)
    inner, outer, source, masked = pl.pallas_call(
        forcing_kernel,
        in_specs=[far] * 4 + [whole(), far, whole()],
        out_specs=[whole()] * 4,
        out_shape=[
            here(REGION, 24, LANES),
            here(REGION, 24, LANES),
            here(*field),
            here(*field),
        ],
        scratch_shapes=[
            pltpu.SMEM(thickness.shape, f32),
            pltpu.SMEM(block_owner.shape, jnp.int32),
            pltpu.SMEM(ocean_counts.shape, jnp.int32),
            pltpu.SMEM(block_mask.shape, jnp.int32),
            here(OWN_ROWS, REGION * LANES),
            here(2, REGION, 24, LANES),
            pltpu.SemaphoreType.DMA((4,)),
            pltpu.SemaphoreType.DMA,
        ],
        compiler_params=params,
        name="forcing",
    )(
        *map(distant, (thickness, block_owner, ocean_counts, block_mask)),
        near(tendency),
        distant(depth),
        near(moved),
    )
    late_two, _ = lax.optimization_barrier((two, inner))
    outer = outer_row_swap(outer)
    inner = inner_swap(inner, "by")
    passed_two = inner_swap(late_two, "by")

    inputs = [near(x) for x in (source, masked, moved, inner, outer, mixed, two, passed_two)]
    source, masked, inner, outer = pl.pallas_call(
        gather_kernel,
        in_specs=[whole(SMEM)] + [whole()] * 8,
        out_specs=[whole()] * 4,
        out_shape=[here(*field), here(*field), here(FOLD, LANES), here(FOLD, LANES)],
        input_output_aliases={1: 0, 2: 1},
        scratch_shapes=[here(2, REGION, 24, LANES), here(2, MOVE, ROWS, LANES)],
        compiler_params=params,
        name="assemble",
    )(block_owner, *inputs)
    inner, outer = inner_swap(inner, "bx"), outer_swap(outer, "bx")

    scales = jnp.asarray(chebyshev_plan()[1], f32)
    heights = pl.pallas_call(
        region_kernel,
        in_specs=[whole(SMEM)] + [whole()] * 2,
        out_specs=whole(),
        out_shape=here(REGION, EXT_ROWS, LANES),
        scratch_shapes=[here(CHUNK, REGION, 8, LANES)] * 7,
        compiler_params=params,
        name="region",
    )(scales, near(source), near(masked))

    inputs = [near(x) for x in (heights, source, masked, inner, outer)]
    heights, first, second = pl.pallas_call(
        sides_kernel,
        in_specs=[whole(SMEM)] * 2 + [whole()] * 5,
        out_specs=[whole()] * 3,
        out_shape=[
            here(REGION, EXT_ROWS, LANES),
            here(MOVE, ROWS, LANES),
            here(MOVE, ROWS, LANES),
        ],
        input_output_aliases={2: 0},
        scratch_shapes=[here(1, PACK_ROWS, LANES)] * 2 + [here(CHUNK, 1, 8, LANES)] * 7,
        compiler_params=params,
        name="sides",
    )(block_owner, scales, *inputs)
    passed = inner_swap(first, "by")
    odd = lax.axis_index("by") % 2 == 1
    back = ring(jnp.where(odd, second + passed, second), -2)

    out, tail = pl.pallas_call(
        write_kernel,
        in_specs=[whole(SMEM), whole()],
        out_specs=[whole()] * 2,
        out_shape=[jax.ShapeDtypeStruct((SLOTS, ROWS, LANES), f32), here(MOVE, ROWS, LANES)],
        compiler_params=params,
        name="write",
    )(block_owner, near(heights))
    return pl.pallas_call(
        tail_kernel,
        in_specs=[far] + [whole()] * 3,
        out_specs=far,
        out_shape=jax.ShapeDtypeStruct((SLOTS, ROWS, LANES), f32),
        input_output_aliases={0: 0},
        scratch_shapes=[here(MOVE, ROWS, LANES), pltpu.SemaphoreType.DMA],
        compiler_params=params,
        name="tail",
    )(out, near(tail), near(passed), near(back))


def solution(mesh):
    placed = (
        P(("bx", "by"), None, None, None),
        P(),
        P("by", "bx"),
        P(),
        P("by", "bx"),
        P("by", "bx"),
    )
    return jax.shard_map(
        on_device,
        mesh=mesh,
        in_specs=placed,
        out_specs=P(("bx", "by"), None, None),
        check_vma=False,
    )
```
